256 devices in a mesh: grp: 64 (over y, z, core), sub: 4 (over x).
Axes of the slice: x: 4, y: 4, z: 8, core: 2. Of those that a mesh axis runs over, the one named last changes fastest.
Arguments:
- adj_next: float32 [64, 128, 128, 128], P('grp', 'sub'), may hold values from -4.5 to 4.5
- adj_later: float32 [64, 128, 128, 128], P('grp', 'sub'), may hold values from -2.25 to 2.25
- box_sizes: int32 [64, 2], replicated, may hold values from 64 to 128, as said below
- holder: int32 [64], replicated, may hold values from 0 to 63, as said below
- partner: int32 [64, 2, 4], replicated, may hold values from -1 to 255, as said below
Outputs:
- adj_now: float32 [64, 128, 128, 128], P('grp', 'sub')
- adj_earlier: float32 [64, 128, 128, 128], P('grp', 'sub')
The draws below stay inside these ranges and needn't reach their ends.
Inputs may be any that keep to these rules, and one draw needn't show every extreme that they name: box_sizes[p] = (Lx, Ly) with 64 <= Lx <= 128 and 64 <= Ly <= 128; some partition has Lx = 128 and Ly = 128, some has Lx = 64, some has Ly = 64. holder names every slot exactly once. The joining is mutual: if partner[p, f, s] = q * 4 + t then partner[q, 1 - f, t] = p * 4 + s, and q differs from p. A face may be joined in part and walled in part; some faces are wholly walls. Over both faces, a partition has at most 3 segments joined to any one other partition, and some pair of partitions has exactly 3.
All inputs are finite; a program needn't handle non-finite values.
Results may differ from the reference program's by a relative error of at most 0.0003.
Values sent between devices are 32-bit elements; how exact they have to be, the bound alone decides.
A program may use at most 128 MiB of HBM per device.

```python
import jax
import jax.numpy as jnp
from jax import lax

PX = 128
Y = 128
Z = 128
SEGS = 4
PARTS_SIZE = 64


def layout(key):
    box_key = jax.random.fold_in(key, 7001)
    key_x, key_y, key_pick = jax.random.split(box_key, 3)
    part_ids = jnp.arange(PARTS_SIZE, dtype=jnp.int32)
    len_x = jax.random.randint(key_x, (PARTS_SIZE,), PX // 2, PX + 1, dtype=jnp.int32)
    len_y = jax.random.randint(key_y, (PARTS_SIZE,), Y // 2, Y + 1, dtype=jnp.int32)
    chosen = jax.random.permutation(key_pick, PARTS_SIZE)
    len_x = jnp.where(part_ids == chosen[0], PX, len_x)
    len_x = jnp.where(part_ids == chosen[1], PX // 2, len_x)
    len_y = jnp.where(part_ids == chosen[0], Y, len_y)
    len_y = jnp.where(part_ids == chosen[2], Y // 2, len_y)
    holder = jax.random.permutation(jax.random.fold_in(key, 7002), PARTS_SIZE).astype(jnp.int32)
    return (len_x.astype(jnp.int32), len_y.astype(jnp.int32), holder)


def draw_box_sizes(key, part):
    len_x, len_y, holder = layout(key)
    return jnp.stack([len_x, len_y], axis=1).astype(jnp.int32)


def draw_holder(key, part):
    len_x, len_y, holder = layout(key)
    return holder


def face_weight(key):
    len_x, len_y, holder = layout(key)
    slot_part = jnp.zeros((PARTS_SIZE,), jnp.int32).at[holder].set(jnp.arange(PARTS_SIZE, dtype=jnp.int32))
    slot_len = len_y[slot_part]
    rows = jnp.arange(Y, dtype=jnp.int32)
    near = (rows[None, :] == 1) | (rows[None, :] == slot_len[:, None] - 2)
    weight = jnp.where(near, jnp.float32(1.0), jnp.float32(0.03))
    return weight[:, None, :, None]


def draw_field(key, salt, amplitude):
    weight = face_weight(key)
    value_key = jax.random.fold_in(key, salt)
    values = jax.random.normal(value_key, (PARTS_SIZE, PX, Y, Z), jnp.float32)
    values = jnp.clip(values, -4.5, 4.5)
    return (amplitude * weight * values).astype(jnp.float32)


def draw_adj_next(key, part):
    return draw_field(key, 7101, 1.0)


def draw_adj_later(key, part):
    return draw_field(key, 7102, 0.5)


def draw_partner(key, part):
    key_order, key_shift, key_wall = jax.random.split(key, 3)
    chain_order = jax.random.permutation(key_order, PARTS_SIZE).astype(jnp.int32)
    seg_shift = jnp.where(jax.random.randint(key_shift, (), 0, 2) == 0, 1, SEGS - 1)
    places = jnp.arange(PARTS_SIZE, dtype=jnp.int32)
    walled = jax.random.randint(key_wall, (PARTS_SIZE,), 0, 4) == 0
    walled = (walled | (places == PARTS_SIZE - 1)) & (places != 0)
    segment = jnp.arange(SEGS, dtype=jnp.int32)
    up_step = 1 + (segment[None, :] >= SEGS - seg_shift).astype(jnp.int32)
    up_part = chain_order[(places[:, None] + up_step) % PARTS_SIZE]
    up_seg = (segment[None, :] + seg_shift) % SEGS
    up_link = jnp.where(walled[:, None], -1, up_part * SEGS + up_seg)
    down_step = 1 + (segment[None, :] < seg_shift).astype(jnp.int32)
    down_place = (places[:, None] - down_step) % PARTS_SIZE
    down_part = chain_order[down_place]
    down_seg = (segment[None, :] - seg_shift) % SEGS
    down_link = jnp.where(walled[down_place], -1, down_part * SEGS + down_seg)
    face_rows = jnp.stack([down_link, up_link], axis=1).astype(jnp.int32)
    return jnp.zeros((PARTS_SIZE, 2, SEGS), jnp.int32).at[chain_order].set(face_rows)


def setup_inputs(seed: int = 0) -> dict:
    splits = jax.random.split(jax.random.key(seed), 6)
    adj_next = draw_adj_next(jax.random.fold_in(splits[5], 71), 0)
    adj_later = draw_adj_later(jax.random.fold_in(splits[5], 71), 0)
    box_sizes = draw_box_sizes(jax.random.fold_in(splits[5], 71), 0)
    holder = draw_holder(jax.random.fold_in(splits[5], 71), 0)
    partner = draw_partner(jax.random.fold_in(splits[5], 71), 0)
    return {"adj_next": adj_next, "adj_later": adj_later, "box_sizes": box_sizes, "holder": holder, "partner": partner}


time_step = 0.5
precise = lax.Precision.HIGHEST
stencil_rows = ((0, 0, -2, 2, 0, 0), (0, 2, -27, 27, -2, 0), (-2, 27, -270, 270, -27, 2), (2, -27, 270, -270, 27, -2), (0, -2, 27, -27, 2, 0), (0, 0, 2, -2, 0, 0))

def cosine_table(size_cells, length):
    mode_index = jnp.arange(size_cells, dtype=jnp.int32)[:, None]
    cell_index = jnp.arange(size_cells, dtype=jnp.int32)[None, :]
    extent = length.astype(jnp.float32)
    angles = jnp.pi * mode_index.astype(jnp.float32) * (cell_index.astype(jnp.float32) + 0.5) / extent
    scaling = jnp.sqrt(jnp.where(mode_index == 0, 1.0, 2.0).astype(jnp.float32) / extent)
    inside = (mode_index < length) & (cell_index < length)
    return jnp.where(inside, scaling * jnp.cos(angles), jnp.float32(0.0)).astype(jnp.float32)

def update_factors(len_x, len_y, first_y, count_y, total_x, total_z):
    wave_x = jnp.arange(total_x, dtype=jnp.int32).astype(jnp.float32) / len_x.astype(jnp.float32)
    wave_y = (first_y + jnp.arange(count_y, dtype=jnp.int32)).astype(jnp.float32) / len_y.astype(jnp.float32)
    wave_z = jnp.arange(total_z, dtype=jnp.int32).astype(jnp.float32) / jnp.float32(total_z)
    angular = jnp.pi * jnp.sqrt(wave_x[:, None, None] ** 2 + wave_y[None, :, None] ** 2 + wave_z[None, None, :] ** 2)
    two_cos = 2.0 * jnp.cos(angular * time_step)
    source = time_step ** 2 * jnp.sinc(angular * (time_step / (2.0 * jnp.pi))) ** 2
    return (two_cos.astype(jnp.float32), source.astype(jnp.float32))

def forward_cosine(physical, table_x, table_y, table_z):
    spectral = jnp.einsum('kx,xyz->kyz', table_x, physical, precision=precise)
    spectral = jnp.einsum('ly,kyz->klz', table_y, spectral, precision=precise)
    return jnp.einsum('mz,klz->klm', table_z, spectral, precision=precise)

def inverse_cosine(spectral, table_x, table_y, table_z):
    physical = jnp.einsum('kx,klm->xlm', table_x, spectral, precision=precise)
    physical = jnp.einsum('ly,xlm->xym', table_y, physical, precision=precise)
    return jnp.einsum('mz,xym->xyz', table_z, physical, precision=precise)

def coupling_terms(own_strips, other_strips):
    weights = jnp.transpose(jnp.asarray(stencil_rows, dtype=jnp.float32)) / 180.0
    low_terms = jnp.einsum('ij,...jw->...iw', weights[3:6, 0:3], other_strips[..., 0, :, :, :], precision=precise) + jnp.einsum('ij,...jw->...iw', weights[3:6, 3:6], own_strips[..., 0, :, :, :], precision=precise)
    high_terms = jnp.einsum('ij,...jw->...iw', weights[0:3, 0:3], own_strips[..., 1, :, :, :], precision=precise) + jnp.einsum('ij,...jw->...iw', weights[0:3, 3:6], other_strips[..., 1, :, :, :], precision=precise)
    return jnp.stack([low_terms, high_terms], axis=-4)

def place_terms(result, low_terms, high_terms, len_y):
    result = result.at[:, 0:3, :].add(low_terms)
    window = lax.dynamic_slice_in_dim(result, len_y - 3, 3, 1)
    return lax.dynamic_update_slice_in_dim(result, window + high_terms, len_y - 3, 1)

def reverse_step(current, earlier, box_sizes, holder, partner, slot_part):
    part_count, x_cells, y_cells, z_cells = current.shape
    seg_count = partner.shape[2]
    seg_cells = z_cells // seg_count

    def per_slot(slot_index):
        owner_part = slot_part[slot_index]
        len_x = box_sizes[owner_part, 0]
        len_y = box_sizes[owner_part, 1]
        table_x = cosine_table(x_cells, len_x)
        table_y = cosine_table(y_cells, len_y)
        table_z = cosine_table(z_cells, jnp.int32(z_cells))
        two_cos, source = update_factors(len_x, len_y, 0, y_cells, x_cells, z_cells)
        spectral = forward_cosine(current[slot_index], table_x, table_y, table_z)
        wave_part = inverse_cosine(two_cos * spectral, table_x, table_y, table_z)
        force_part = inverse_cosine(source * spectral, table_x, table_y, table_z)
        low_rows = force_part[:, 0:3, :]
        high_rows = lax.dynamic_slice_in_dim(force_part, len_y - 3, 3, 1)
        return (wave_part, jnp.stack([low_rows, high_rows]))
    wave_all, strip_all = lax.map(per_slot, jnp.arange(part_count, dtype=jnp.int32))
    own_all = strip_all.reshape(part_count, 2, x_cells, 3, seg_count, seg_cells)
    own_all = jnp.transpose(own_all, (0, 1, 4, 3, 2, 5)).reshape(part_count, 2, seg_count, 3, x_cells * seg_cells)
    link_ids = partner[slot_part]
    is_wall = link_ids < 0
    safe_links = jnp.maximum(link_ids, 0)
    peer_part = safe_links // seg_count
    peer_seg = safe_links % seg_count
    peer_slot = holder[peer_part]
    peer_face = jnp.broadcast_to(1 - jnp.arange(2, dtype=jnp.int32)[None, :, None], link_ids.shape)
    other_all = own_all[peer_slot, peer_face, peer_seg]
    coupled = coupling_terms(own_all, other_all)
    len_x_all = box_sizes[slot_part, 0]
    len_y_all = box_sizes[slot_part, 1]
    x_limit = jnp.minimum(len_x_all[:, None, None], box_sizes[peer_part, 0])
    column_x = jnp.arange(x_cells * seg_cells, dtype=jnp.int32) // seg_cells
    joined = ((column_x < x_limit[..., None]) & jnp.logical_not(is_wall)[..., None]).astype(jnp.float32)
    coupled = coupled * joined[:, :, :, None, :]
    coupled = coupled.reshape(part_count, 2, seg_count, 3, x_cells, seg_cells)
    coupled = jnp.transpose(coupled, (0, 1, 4, 3, 2, 5)).reshape(part_count, 2, x_cells, 3, z_cells)
    x_index = jnp.arange(x_cells, dtype=jnp.int32)
    y_index = jnp.arange(y_cells, dtype=jnp.int32)
    inside = ((x_index[None, :, None, None] < len_x_all[:, None, None, None]) & (y_index[None, None, :, None] < len_y_all[:, None, None, None])).astype(jnp.float32)
    result = wave_all - inside * earlier
    return jax.vmap(place_terms)(result, coupled[:, 0], coupled[:, 1], len_y_all)

def reference(adj_next, adj_later, box_sizes, holder, partner):
    part_count = holder.shape[0]
    slot_part = jnp.zeros((part_count,), jnp.int32).at[holder].set(jnp.arange(part_count, dtype=jnp.int32))
    adj_now = reverse_step(adj_next, adj_later, box_sizes, holder, partner, slot_part)
    adj_earlier = reverse_step(adj_now, adj_next, box_sizes, holder, partner, slot_part)
    return (adj_now, adj_earlier)
```

```python
import jax
import jax.numpy as jnp
from jax import lax
from jax.sharding import Mesh
from jax.sharding import PartitionSpec as P

time_step = 0.5
precise = lax.Precision.HIGH
stencil_rows = (
    (0, 0, -2, 2, 0, 0),
    (0, 2, -27, 27, -2, 0),
    (-2, 27, -270, 270, -27, 2),
    (2, -27, 270, -270, 27, -2),
    (0, -2, 27, -27, 2, 0),
    (0, 0, 2, -2, 0, 0),
)


def cosine_table(size_cells, length):
    mode_index = jnp.arange(size_cells, dtype=jnp.int32)[:, None]
    cell_index = jnp.arange(size_cells, dtype=jnp.int32)[None, :]
    extent = length.astype(jnp.float32)
    angles = (
        jnp.pi * mode_index.astype(jnp.float32) * (cell_index.astype(jnp.float32) + 0.5) / extent
    )
    scaling = jnp.sqrt(jnp.where(mode_index == 0, 1.0, 2.0).astype(jnp.float32) / extent)
    inside = (mode_index < length) & (cell_index < length)
    return jnp.where(inside, scaling * jnp.cos(angles), jnp.float32(0.0))


def plane_inverse(spectral, table_y, table_z):
    physical = jnp.einsum("ly,xlm->xym", table_y, spectral, precision=precise)
    return jnp.einsum("mz,xym->xyz", table_z, physical, precision=precise)


def coupling_terms(own_strips, other_strips):
    weights = jnp.transpose(jnp.asarray(stencil_rows, dtype=jnp.float32)) / 180.0
    low_terms = jnp.einsum(
        "ij,...jw->...iw", weights[3:6, 0:3], other_strips[..., 0, :, :, :], precision=precise
    ) + jnp.einsum(
        "ij,...jw->...iw", weights[3:6, 3:6], own_strips[..., 0, :, :, :], precision=precise
    )
    high_terms = jnp.einsum(
        "ij,...jw->...iw", weights[0:3, 0:3], own_strips[..., 1, :, :, :], precision=precise
    ) + jnp.einsum(
        "ij,...jw->...iw", weights[0:3, 3:6], other_strips[..., 1, :, :, :], precision=precise
    )
    return jnp.stack([low_terms, high_terms], axis=-4)


def to_segments(strip_rows, pieces):
    x_cells, row_count, z_cells = strip_rows.shape
    layered = strip_rows.reshape(x_cells, row_count, pieces, z_cells // pieces)
    return jnp.transpose(layered, (2, 1, 0, 3)).reshape(
        pieces, row_count, x_cells * (z_cells // pieces)
    )


def from_segments(values, x_cells):
    pieces, row_count, flat_width = values.shape
    layered = values.reshape(pieces, row_count, x_cells, flat_width // x_cells)
    return jnp.transpose(layered, (2, 1, 0, 3)).reshape(
        x_cells, row_count, pieces * (flat_width // x_cells)
    )


sinc_terms = (1.0, -1.0 / 6, 1.0 / 120, -1.0 / 5040, 1.0 / 362880, -1.0 / 39916800, 1.0 / 6227020800)


def update_factors(len_x, len_y, first_y, count_y, total_x, total_z):
    wave_x = jnp.arange(total_x, dtype=jnp.int32).astype(jnp.float32) / len_x.astype(jnp.float32)
    wave_y = (first_y + jnp.arange(count_y, dtype=jnp.int32)).astype(jnp.float32) / len_y.astype(
        jnp.float32
    )
    wave_z = jnp.arange(total_z, dtype=jnp.int32).astype(jnp.float32) / jnp.float32(total_z)
    quarter = jnp.float32((jnp.pi * time_step / 2) ** 2)
    square = quarter * (
        wave_x[:, None, None] ** 2 + wave_y[None, :, None] ** 2 + wave_z[None, None, :] ** 2
    )
    series = jnp.full_like(square, sinc_terms[-1])
    for term in sinc_terms[-2::-1]:
        series = series * square + jnp.float32(term)
    unit = series * series
    return 2.0 - 4.0 * square * unit, time_step**2 * unit


def local(adj_next, adj_later, box_sizes, holder, partner):
    part_count = holder.shape[0]
    seg_count = partner.shape[2]
    item_count = 2 * seg_count
    rows = lax.axis_size("row")
    plane = lax.axis_size("plane")
    my_row = lax.axis_index("row")
    my_place = lax.axis_index("plane")
    my_group = my_row * plane + my_place
    my_column = lax.axis_index("sub")
    sub_count = lax.axis_size("sub")
    x_local = adj_next.shape[1]
    y_cells = adj_next.shape[2]
    z_cells = adj_next.shape[3]
    x_total = x_local * sub_count
    y_local = y_cells // sub_count
    seg_cells = z_cells // seg_count
    strip_width = x_local * seg_cells
    part_ids = jnp.arange(part_count, dtype=jnp.int32)
    groups = jnp.arange(rows, dtype=jnp.int32) * plane + my_place
    row_parts = jnp.sum(jnp.where(holder[None, :] == groups[:, None], part_ids[None, :], 0), axis=1)
    my_part = jnp.sum(jnp.where(holder == my_group, part_ids, 0))
    len_x = box_sizes[my_part, 0]
    len_y = box_sizes[my_part, 1]
    table_x = cosine_table(x_total, len_x)
    table_y = cosine_table(y_cells, len_y)
    table_z = cosine_table(z_cells, jnp.int32(z_cells))
    face_table = jnp.concatenate(
        [table_y[:, 0:3], lax.dynamic_slice_in_dim(table_y, len_y - 3, 3, 1)], axis=1
    )
    my_face = lax.dynamic_slice_in_dim(face_table, my_column * y_local, y_local, 0)
    two_cos, source = update_factors(len_x, len_y, my_column * y_local, y_local, x_total, z_cells)
    x_global = my_column * x_local + jnp.arange(x_local, dtype=jnp.int32)
    y_index = jnp.arange(y_cells, dtype=jnp.int32)
    inside = ((x_global[:, None, None] < len_x) & (y_index[None, :, None] < len_y)).astype(
        jnp.float32
    )
    item_ids = jnp.arange(item_count, dtype=jnp.int32)
    link_ids = partner[row_parts].reshape(rows, item_count)
    safe_links = jnp.maximum(link_ids, 0)
    peer_group = holder[safe_links // seg_count]
    peer_item = (1 - item_ids // seg_count)[None, :] * seg_count + safe_links % seg_count
    pick = (peer_group % plane) * item_count + peer_item
    pick_here = (peer_group // plane == my_row).astype(jnp.float32)[:, :, None, None]
    my_links = partner[my_part].reshape(item_count)
    x_limit = jnp.minimum(len_x, box_sizes[jnp.maximum(my_links, 0) // seg_count, 0])
    column_x = my_column * x_local + jnp.arange(strip_width, dtype=jnp.int32) // seg_cells
    joined = ((column_x[None, :] < x_limit[:, None]) & (my_links >= 0)[:, None]).astype(
        jnp.float32
    )
    joined = joined.reshape(2, seg_count, 1, strip_width)

    def to_modes(field):
        spectral = jnp.einsum("mz,xyz->xym", table_z, field, precision=precise)
        spectral = jnp.einsum("ly,xym->xlm", table_y, spectral, precision=precise)
        spectral = lax.all_to_all(spectral, "sub", split_axis=1, concat_axis=0, tiled=True)
        return jnp.einsum("kx,xlm->klm", table_x, spectral, precision=precise)

    def to_cells(modes):
        field = jnp.einsum("kx,klm->xlm", table_x, modes, precision=precise)
        field = lax.all_to_all(field, "sub", split_axis=0, concat_axis=1, tiled=True)
        return plane_inverse(field, table_y, table_z)

    def coupling(modes):
        faces = jnp.einsum("lr,klm->rkm", my_face, source * modes, precision=precise)
        faces = jnp.einsum("kx,rkm->rxm", table_x, faces, precision=precise)
        faces = faces.reshape(6, sub_count, x_local, z_cells)
        faces = lax.all_to_all(faces, "sub", split_axis=1, concat_axis=1, tiled=True)
        faces = jnp.sum(faces, axis=1)
        faces = jnp.einsum("mz,rxm->xrz", table_z, faces, precision=precise)
        own_strips = jnp.concatenate(
            [to_segments(faces[:, 0:3], seg_count), to_segments(faces[:, 3:6], seg_count)], axis=0
        )
        nearby = lax.all_gather(own_strips, "plane", axis=0, tiled=True)
        wanted = nearby[pick] * pick_here
        other_strips = lax.all_to_all(wanted, "row", split_axis=0, concat_axis=0, tiled=True)
        other_strips = jnp.sum(other_strips, axis=0)
        coupled = coupling_terms(
            own_strips.reshape(2, seg_count, 3, strip_width),
            other_strips.reshape(2, seg_count, 3, strip_width),
        )
        coupled = coupled * joined
        return from_segments(coupled[0], x_local), from_segments(coupled[1], x_local)

    def place(result, terms):
        result = result.at[:, 0:3, :].add(terms[0])
        window = lax.dynamic_slice_in_dim(result, len_y - 3, 3, 1)
        return lax.dynamic_update_slice_in_dim(result, window + terms[1], len_y - 3, 1)

    modes_next = to_modes(adj_next[0])
    modes_later = to_modes(adj_later[0])
    terms_next = coupling(modes_next)
    adj_now = place(to_cells(two_cos * modes_next) - inside * adj_later[0], terms_next)
    term_rows = jnp.concatenate(terms_next, axis=1)
    term_rows = jnp.einsum("mz,xrz->rxm", table_z, term_rows, precision=precise)
    term_rows = lax.all_gather(term_rows, "sub", axis=1, tiled=True)
    term_rows = jnp.einsum("kx,rxm->rkm", table_x, term_rows, precision=precise)
    modes_now = two_cos * modes_next - modes_later
    modes_now = modes_now + jnp.einsum("lr,rkm->klm", my_face, term_rows, precision=precise)
    terms_now = coupling(modes_now)
    adj_earlier = place(to_cells(two_cos * modes_now) - inside * adj_next[0], terms_now)
    return (adj_now[None], adj_earlier[None])


def solution(mesh):
    rows = 4
    devices = mesh.devices
    split = Mesh(devices.reshape(rows, devices.shape[0] // rows, devices.shape[1]), ("row", "plane", "sub"))
    field = P(("row", "plane"), "sub", None, None)
    return jax.shard_map(
        local,
        mesh=split,
        in_specs=(field, field, P(), P(), P()),
        out_specs=(field, field),
        check_vma=False,
    )
```

```python
import functools

import jax
import jax.numpy as jnp
from jax import lax
from jax.experimental import pallas as pl
from jax.experimental.pallas import tpu as pltpu
from jax.sharding import Mesh
from jax.sharding import PartitionSpec as P

time_step = 0.5
stencil_rows = (
    (0, 0, -2, 2, 0, 0),
    (0, 2, -27, 27, -2, 0),
    (-2, 27, -270, 270, -27, 2),
    (2, -27, 270, -270, 27, -2),
    (0, -2, 27, -27, 2, 0),
    (0, 0, 2, -2, 0, 0),
)
weights = [[stencil_rows[j][i] / 180.0 for j in range(6)] for i in range(6)]
sinc_terms = (1.0, -1.0 / 6, 1.0 / 120, -1.0 / 5040, 1.0 / 362880, -1.0 / 39916800, 1.0 / 6227020800)
MESH = pl.DeviceIdType.MESH
N = 128
X = 32
CHUNKS = 4
CX = X // CHUNKS
ROWS, RING, CORES, SUBS = 4, 8, 2, 4
f32 = jnp.float32
bf16 = jnp.bfloat16


def cosine_table(size_cells, length):
    mode_index = jnp.arange(size_cells, dtype=jnp.int32)[:, None]
    cell_index = jnp.arange(size_cells, dtype=jnp.int32)[None, :]
    extent = length.astype(jnp.float32)
    angles = (
        jnp.pi * mode_index.astype(jnp.float32) * (cell_index.astype(jnp.float32) + 0.5) / extent
    )
    scaling = jnp.sqrt(jnp.where(mode_index == 0, 1.0, 2.0).astype(jnp.float32) / extent)
    inside = (mode_index < length) & (cell_index < length)
    return jnp.where(inside, scaling * jnp.cos(angles), jnp.float32(0.0))


def parts_of(value):
    high = value.astype(bf16)
    return high, (value - high.astype(f32)).astype(bf16)


def left_stack(table):
    high, low = parts_of(table)
    return jnp.concatenate(
        [jnp.concatenate([high, high], 1), jnp.concatenate([low, jnp.zeros_like(low)], 1)], 0
    )


def right_stack(table):
    high, low = parts_of(table)
    return jnp.concatenate(
        [jnp.concatenate([high, low], 1), jnp.concatenate([high, jnp.zeros_like(low)], 1)], 0
    )


def times_right(value, stack):
    high, low = parts_of(value)
    out = jnp.dot(jnp.concatenate([high, low], 1), stack, preferred_element_type=f32)
    return out[:, :N] + out[:, N:]


def left_times(stack, pair):
    high, low = parts_of(pair)
    out = jnp.dot(stack, jnp.concatenate([high, low], 0), preferred_element_type=f32)
    return out[:N] + out[N:]


def kernel(
    ints, floats, adj_next, adj_later, tables, base, limits,
    out_now, out_earlier,
    fields, stage, recv, back, land, stacks, modes, wave, source,
    faces, face_send, face_in, near_first, near_second, wanted, wanted_in, coup, coup_send, coup_all, coup_modes,
    load_sem, store_sem, local_sem, big_send, big_recv,
    face_ssem, face_rsem, ring_ssem, ring_rsem, core_ssem, core_rsem,
    row_ssem, row_rsem, all_ssem, all_rsem,
):
    row, ring = lax.axis_index("row"), lax.axis_index("z")
    core, sub = lax.axis_index("core"), lax.axis_index("sub")
    inputs = (adj_next, adj_later)
    outputs = (out_now, out_earlier)
    recv_flat = [recv.at[i].reshape(N * X, N) for i in range(2)]
    back_flat = [back.at[i].reshape(N * X, N) for i in range(2)]
    near = (near_first, near_second)
    sent = []

    def load(i, c):
        return pltpu.make_async_copy(
            inputs[i].at[0, pl.ds(CX * c, CX)], fields.at[i, pl.ds(CX * c, CX)], load_sem.at[i, c]
        )

    for i in range(2):
        for c in range(CHUNKS):
            load(i, c).start()

    barrier = pltpu.get_barrier_semaphore()
    for j in (1, 2, 3):
        pl.semaphore_signal(barrier, inc=1, device_id={"sub": lax.rem(sub + j, SUBS)}, device_id_type=MESH)
        pl.semaphore_signal(barrier, inc=1, device_id={"row": lax.rem(row + j, ROWS)}, device_id_type=MESH)
    for j in (1, RING - 1):
        pl.semaphore_signal(barrier, inc=1, device_id={"z": lax.rem(ring + j, RING)}, device_id_type=MESH)
    pl.semaphore_signal(barrier, inc=1, device_id={"core": 1 - core}, device_id_type=MESH)

    for i in range(4):
        stacks[i] = left_stack(tables[i])
    for i in (4, 5):
        stacks[i] = right_stack(tables[i])
    pl.semaphore_wait(barrier, 9)

    def remote(src, dst, ssem, rsem, where):
        copy = pltpu.make_async_remote_copy(
            src_ref=src, dst_ref=dst, send_sem=ssem, recv_sem=rsem, device_id=where, device_id_type=MESH
        )
        return copy

    def post(copy):
        copy.start()
        sent.append(copy)

    def large(a, c, j):
        d = lax.rem(sub + j, SUBS)
        if a < 2:
            src = stage.at[a, pl.ds(CX * c, CX), pl.ds(X * d, X), :]
            dst = recv.at[a, pl.ds(X * sub + CX * c, CX)]
        else:
            src = back.at[a - 2, pl.ds(X * d + CX * c, CX)]
            dst = land.at[a - 2, pl.ds(CX * c, CX), pl.ds(X * sub, X), :]
        return src, dst, d

    def large_copy(a, c, j):
        src, dst, d = large(a, c, j)
        if j == 0:
            return pltpu.make_async_copy(src, dst, local_sem.at[a, c])
        return remote(src, dst, big_send.at[a, c, j - 1], big_recv.at[a, c, j - 1], {"sub": d})

    def large_start(a, c):
        for j in (2, 1, 3):
            post(large_copy(a, c, j))
        large_copy(a, c, 0).start()

    def large_wait(a, c):
        large_copy(a, c, 0).wait()
        for j in (1, 3, 2):
            large_copy(a, c, j).wait_recv()

    def forward_chunk(i, c):
        def step(p, carry):
            x0 = CX * c + 2 * p
            value = times_right(fields[i, pl.ds(x0, 2)].reshape(2 * N, N), stacks[4])
            value = left_times(stacks[2], jnp.concatenate([value[:N], value[N:]], 1))
            stage[i, x0] = value[:, :N]
            stage[i, x0 + 1] = value[:, N:]
            return carry

        lax.fori_loop(0, CX // 2, step, 0, unroll=2)

    def to_modes(i, l0):
        pair = jnp.concatenate(
            [
                recv_flat[i][pl.ds(l0, N, stride=X), :],
                recv_flat[i][pl.ds(l0 + 1, N, stride=X), :],
            ],
            1,
        )
        return left_times(stacks[0], pair)

    def from_modes(i, l0, pair):
        value = left_times(stacks[1], pair)
        back_flat[i][pl.ds(l0, N, stride=X), :] = value[:, :N]
        back_flat[i][pl.ds(l0 + 1, N, stride=X), :] = value[:, N:]

    def add_faces(l0, first, second):
        for r in range(6):
            faces[r] = faces[r] + (floats[X + 6 * l0 + r] * first + floats[X + 6 * l0 + 6 + r] * second)

    def face_copy(e, j):
        d = lax.rem(sub + j, SUBS)
        return remote(
            face_send.at[e, :, pl.ds(X * d, X), :],
            face_in.at[e, j - 1],
            face_ssem.at[e, j - 1],
            face_rsem.at[e, j - 1],
            {"sub": d},
        )

    def faces_start(e):
        for r in (0, 2, 4):
            value = left_times(stacks[1], jnp.concatenate([faces[r], faces[r + 1]], 1))
            face_send[e, r] = value[:, :N]
            face_send[e, r + 1] = value[:, N:]
        for j in (2, 1, 3):
            post(face_copy(e, j))

    def slot(k):
        return lax.rem(ring + k + RING, RING) * CORES + core

    def ring_copy(e, h, side):
        owner = -(h - 1) if side == 0 else h - 1
        k = h - 1 if side == 0 else 3 + h
        block = near[e].at[slot(owner)]
        target = lax.rem(ring + (1 if side == 0 else RING - 1), RING)
        return remote(block, block, ring_ssem.at[e, k], ring_rsem.at[e, k], {"z": target})

    def core_copy(e, k):
        owner = -k if k < 5 else k - 4
        block = near[e].at[slot(owner)]
        return remote(block, block, core_ssem.at[e, k], core_rsem.at[e, k], {"core": 1 - core})

    def row_copy(e, j):
        return remote(
            wanted.at[e, j],
            wanted_in.at[e, j - 1],
            row_ssem.at[e, j - 1],
            row_rsem.at[e, j - 1],
            {"row": lax.rem(row + j, ROWS)},
        )

    def exchange(e, fill):
        fill = list(fill)

        def other_work():
            if fill:
                fill.pop(0)()

        other_work()
        for j in (1, 3, 2):
            face_copy(e, j).wait_recv()
        own = face_send[e, :, pl.ds(X * sub, X), :] + face_in[e, 0] + face_in[e, 1] + face_in[e, 2]
        own = times_right(own.reshape(6 * X, N), stacks[5]).reshape(6, X, N)
        near[e][slot(0)] = own
        post(ring_copy(e, 1, 0))
        post(ring_copy(e, 1, 1))
        post(core_copy(e, 0))
        for h in (1, 2, 3, 4):
            other_work()
            ring_copy(e, h, 0).wait_recv()
            if h < 4:
                post(ring_copy(e, h + 1, 0))
            post(core_copy(e, h))
            if h < 4:
                ring_copy(e, h, 1).wait_recv()
                if h < 3:
                    post(ring_copy(e, h + 1, 1))
                post(core_copy(e, 4 + h))
        other_work()
        for k in range(8):
            core_copy(e, k).wait_recv()

        lane = lax.broadcasted_iota(jnp.int32, (3, X, N), 2) // (N // 4)

        def choose(j, carry):
            for face in range(2):
                total = jnp.zeros((3, X, N), f32)
                for seg in range(4):
                    at = 2 + 3 * (8 * j + 4 * face + seg)
                    value = near[e][ints[at], 3 * (1 - face) : 3 * (1 - face) + 3]
                    shift = jnp.full((3, X, N), ints[at + 1], jnp.int32)
                    value = jnp.where(shift % 2 == 1, pltpu.roll(value, N // 4, 2), value)
                    value = jnp.where(shift >= 2, pltpu.roll(value, N // 2, 2), value)
                    taken = (lane == seg) & (jnp.full((3, X, N), ints[at + 2], jnp.int32) == 1)
                    total = jnp.where(taken, value, total)
                wanted[e, j, 3 * face : 3 * face + 3] = total
            return carry

        lax.fori_loop(0, ROWS, choose, 0)
        for j in (2, 1, 3):
            post(row_copy(e, j))
        for work in fill:
            work()
        for j in (1, 3, 2):
            row_copy(e, j).wait_recv()
        other = wanted[e, 0] + wanted_in[e, 0] + wanted_in[e, 1] + wanted_in[e, 2]
        own = near[e][slot(0)]
        x_here = (sub * X + lax.broadcasted_iota(jnp.int32, (X, N), 0)).astype(f32)
        for face in range(2):
            limit = jnp.broadcast_to(limits[pl.ds(face, 1), :], (X, N))
            joined = x_here < limit
            values = [other[0], other[1], other[2], own[0], own[1], own[2]]
            if face == 1:
                values = [own[3], own[4], own[5], other[3], other[4], other[5]]
            for i in range(3):
                line = weights[3 * (1 - face) + i]
                term = sum(line[k] * values[k] for k in range(6) if line[k] != 0.0)
                coup[e, 3 * face + i] = jnp.where(joined, term, 0.0)

    len_x, len_y = ints[0], ints[1]
    y_index = lax.broadcasted_iota(jnp.int32, (N, N), 0)
    face_rows = [0, 1, 2, len_y - 3, len_y - 2, len_y - 1]

    def finish_chunk(i, c):
        def step(p, carry):
            x0 = CX * c + 2 * p
            value = left_times(stacks[3], jnp.concatenate([land[i, x0], land[i, x0 + 1]], 1))
            value = times_right(jnp.concatenate([value[:, :N], value[:, N:]], 0), stacks[5])
            for q in range(2):
                x = x0 + q
                result = value[N * q : N * q + N]
                inside = (y_index < len_y) & (jnp.full((N, N), sub * X + x, jnp.int32) < len_x)
                result = result - jnp.where(inside, fields[1 - i, x], 0.0)
                extra = jnp.zeros((N, N), f32)
                for r in range(6):
                    line = jnp.broadcast_to(coup[i, r, pl.ds(x, 1), :], (N, N))
                    extra = jnp.where(y_index == face_rows[r], line, extra)
                land[i, x] = result + extra
            return carry

        lax.fori_loop(0, CX // 2, step, 0, unroll=2)
        store(i, c).start()

    def store(i, c):
        return pltpu.make_async_copy(
            land.at[i, pl.ds(CX * c, CX)], outputs[i].at[0, pl.ds(CX * c, CX)], store_sem.at[i, c]
        )

    for c in range(CHUNKS):
        load(0, c).wait()
        forward_chunk(0, c)
        large_start(0, c)
    for c in range(CHUNKS):
        load(1, c).wait()
        forward_chunk(1, c)
        if c == 0:
            large_start(1, 0)

    def factors(l, carry):
        square = base[...] + floats[l]
        series = jnp.full((N, N), sinc_terms[-1], f32)
        for term in sinc_terms[-2::-1]:
            series = series * square + f32(term)
        unit = series * series
        wave[l] = 2.0 - 4.0 * (square * unit)
        source[l] = time_step**2 * unit
        return carry

    lax.fori_loop(0, X, factors, 0, unroll=2)
    for r in range(6):
        faces[r] = jnp.zeros((N, N), f32)
    for c in range(CHUNKS):
        large_wait(0, c)

    def first_modes(p, carry):
        l0 = 2 * p
        value = to_modes(0, l0)
        modes[0, l0] = value[:, :N]
        modes[0, l0 + 1] = value[:, N:]
        add_faces(l0, source[l0] * value[:, :N], source[l0 + 1] * value[:, N:])
        return carry

    lax.fori_loop(0, X // 2, first_modes, 0, unroll=2)
    faces_start(0)
    large_start(1, 1)

    def first_back(p, carry):
        l0 = 2 * p
        pair = jnp.concatenate([wave[l0] * modes[0, l0], wave[l0 + 1] * modes[0, l0 + 1]], 1)
        from_modes(0, l0, pair)
        return carry

    lax.fori_loop(0, X // 2, first_back, 0, unroll=2)

    def start(a, c):
        return lambda: large_start(a, c)

    def later_modes():
        for c in range(CHUNKS):
            large_wait(1, c)

        def step(p, carry):
            l0 = 2 * p
            value = to_modes(1, l0)
            modes[1, l0] = value[:, :N]
            modes[1, l0 + 1] = value[:, N:]
            return carry

        lax.fori_loop(0, X // 2, step, 0, unroll=2)

    exchange(
        0,
        [start(1, 2), start(1, 3), start(2, 0), start(2, 1), start(2, 2), start(2, 3), later_modes],
    )

    def all_copy(j):
        return remote(
            coup_send,
            coup_all.at[:, pl.ds(X * sub, X), :],
            all_ssem.at[j - 1],
            all_rsem.at[j - 1],
            {"sub": lax.rem(sub + j, SUBS)},
        )

    coup_rows = times_right(coup[0].reshape(6 * X, N), stacks[4]).reshape(6, X, N)
    coup_send[...] = coup_rows
    coup_all[:, pl.ds(X * sub, X), :] = coup_rows
    for j in (2, 1, 3):
        post(all_copy(j))
    for r in range(6):
        faces[r] = jnp.zeros((N, N), f32)
    for j in (1, 3, 2):
        all_copy(j).wait_recv()
    for r in (0, 2, 4):
        value = left_times(stacks[0], jnp.concatenate([coup_all[r], coup_all[r + 1]], 1))
        coup_modes[r] = value[:, :N]
        coup_modes[r + 1] = value[:, N:]

    def second_modes(p, carry):
        l0 = 2 * p
        pair = []
        for q in range(2):
            l = l0 + q
            value = wave[l] * modes[0, l] - modes[1, l]
            for r in range(6):
                value = value + floats[X + 6 * l + r] * coup_modes[r]
            modes[1, l] = value
            pair.append(value)
        add_faces(l0, source[l0] * pair[0], source[l0 + 1] * pair[1])
        return carry

    lax.fori_loop(0, X // 2, second_modes, 0)
    faces_start(1)

    def second_back(p, carry):
        l0 = 2 * p
        pair = jnp.concatenate([wave[l0] * modes[1, l0], wave[l0 + 1] * modes[1, l0 + 1]], 1)
        from_modes(1, l0, pair)
        return carry

    lax.fori_loop(0, X // 2, second_back, 0, unroll=2)
    for c in range(CHUNKS):
        large_start(3, c)

    def finish(i, c):
        def work():
            large_wait(2 + i, c)
            finish_chunk(i, c)

        return work

    exchange(1, [finish(0, 0), finish(0, 1), finish(0, 2), finish(0, 3)])
    for c in range(CHUNKS):
        finish(1, c)()
    for copy in sent:
        copy.wait_send()
    for i in range(2):
        for c in range(CHUNKS):
            store(i, c).wait()


def local(adj_next, adj_later, box_sizes, holder, partner):
    part_count = holder.shape[0]
    seg_count = partner.shape[2]
    item_count = 2 * seg_count
    plane = RING * CORES
    my_row = lax.axis_index("row")
    my_place = lax.axis_index("z") * CORES + lax.axis_index("core")
    my_column = lax.axis_index("sub")
    part_ids = jnp.arange(part_count, dtype=jnp.int32)
    row_ids = (my_row + jnp.arange(ROWS, dtype=jnp.int32)) % ROWS
    groups = row_ids * plane + my_place
    row_parts = jnp.sum(jnp.where(holder[None, :] == groups[:, None], part_ids[None, :], 0), axis=1)
    my_part = row_parts[0]
    len_x = box_sizes[my_part, 0]
    len_y = box_sizes[my_part, 1]
    table_x = cosine_table(N, len_x)
    table_y = cosine_table(N, len_y)
    table_z = cosine_table(N, jnp.int32(N))
    tables = jnp.stack([table_x, table_x.T, table_y, table_y.T, table_z.T, table_z])
    my_modes = lax.dynamic_slice_in_dim(table_y, my_column * X, X, 0)
    my_face = jnp.concatenate(
        [my_modes[:, 0:3], lax.dynamic_slice_in_dim(my_modes, len_y - 3, 3, 1)], axis=1
    )
    count = jnp.arange(N, dtype=jnp.int32).astype(f32)
    quarter = f32((jnp.pi * time_step / 2) ** 2)
    square_x = quarter * (count / len_x.astype(f32)) ** 2
    square_z = quarter * (count / f32(N)) ** 2
    mode_y = (my_column * X + jnp.arange(X, dtype=jnp.int32)).astype(f32)
    square_y = quarter * (mode_y / len_y.astype(f32)) ** 2
    base = square_x[:, None] + square_z[None, :]
    floats = jnp.concatenate([square_y, my_face.reshape(-1)])
    item_ids = jnp.arange(item_count, dtype=jnp.int32)
    link_ids = partner[row_parts].reshape(ROWS, item_count)
    safe_links = jnp.maximum(link_ids, 0)
    peer_part = safe_links // seg_count
    peer_seg = safe_links % seg_count
    peer_group = holder[peer_part]
    shift = (item_ids[None, :] % seg_count - peer_seg) % seg_count
    here = (peer_group // plane == my_row) & (link_ids >= 0)
    picks = jnp.stack([peer_group % plane, shift, here.astype(jnp.int32)], axis=-1)
    ints = jnp.concatenate([jnp.stack([len_x, len_y]), picks.reshape(-1)])
    x_limit = jnp.where(link_ids[0] >= 0, jnp.minimum(len_x, box_sizes[peer_part[0], 0]), 0)
    limits = jnp.repeat(x_limit.reshape(2, seg_count), N // seg_count, axis=1).astype(f32)
    limits = jnp.concatenate([limits, jnp.zeros((6, N), f32)], axis=0)

    vmem = pl.BlockSpec(memory_space=pltpu.VMEM)
    smem = pl.BlockSpec(memory_space=pltpu.SMEM)
    anywhere = pl.BlockSpec(memory_space=pl.ANY)
    block = jax.ShapeDtypeStruct((1, X, N, N), f32)
    dma = pltpu.SemaphoreType.DMA
    return pl.pallas_call(
        kernel,
        out_shape=(block, block),
        in_specs=[smem, smem, anywhere, anywhere, vmem, vmem, vmem],
        out_specs=(anywhere, anywhere),
        scratch_shapes=[
            pltpu.VMEM((2, X, N, N), f32),
            pltpu.VMEM((2, X, N, N), f32),
            pltpu.VMEM((2, N, X, N), f32),
            pltpu.VMEM((2, N, X, N), f32),
            pltpu.VMEM((2, X, N, N), f32),
            pltpu.VMEM((6, 2 * N, 2 * N), bf16),
            pltpu.VMEM((2, X, N, N), f32),
            pltpu.VMEM((X, N, N), f32),
            pltpu.VMEM((X, N, N), f32),
            pltpu.VMEM((6, N, N), f32),
            pltpu.VMEM((2, 6, N, N), f32),
            pltpu.VMEM((2, 3, 6, X, N), f32),
            pltpu.VMEM((plane, 6, X, N), f32),
            pltpu.VMEM((plane, 6, X, N), f32),
            pltpu.VMEM((2, ROWS, 6, X, N), f32),
            pltpu.VMEM((2, 3, 6, X, N), f32),
            pltpu.VMEM((2, 6, X, N), f32),
            pltpu.VMEM((6, X, N), f32),
            pltpu.VMEM((6, N, N), f32),
            pltpu.VMEM((6, N, N), f32),
            dma((2, CHUNKS)),
            dma((2, CHUNKS)),
            dma((4, CHUNKS)),
            dma((4, CHUNKS, 3)),
            dma((4, CHUNKS, 3)),
            dma((2, 3)),
            dma((2, 3)),
            dma((2, 7)),
            dma((2, 7)),
            dma((2, 8)),
            dma((2, 8)),
            dma((2, 3)),
            dma((2, 3)),
            dma((3,)),
            dma((3,)),
        ],
        compiler_params=pltpu.CompilerParams(
            collective_id=0, has_side_effects=True, vmem_limit_bytes=64 * 1000 * 1000
        ),
        name="two_steps",
    )(ints, floats, adj_next, adj_later, tables, base, limits)


def solution(mesh):
    devices = mesh.devices
    split = Mesh(devices.reshape(ROWS, RING, CORES, SUBS), ("row", "z", "core", "sub"))
    field = P(("row", "z", "core"), "sub", None, None)
    return jax.shard_map(
        local,
        mesh=split,
        in_specs=(field, field, P(), P(), P()),
        out_specs=(field, field),
        check_vma=False,
    )
```

```python
import functools

import jax
import jax.numpy as jnp
from jax import lax
from jax.experimental import pallas as pl
from jax.experimental.pallas import tpu as pltpu
from jax.sharding import Mesh
from jax.sharding import PartitionSpec as P

time_step = 0.5
stencil_rows = (
    (0, 0, -2, 2, 0, 0),
    (0, 2, -27, 27, -2, 0),
    (-2, 27, -270, 270, -27, 2),
    (2, -27, 270, -270, 27, -2),
    (0, -2, 27, -27, 2, 0),
    (0, 0, 2, -2, 0, 0),
)
weights = [[stencil_rows[j][i] / 180.0 for j in range(6)] for i in range(6)]
sinc_terms = (1.0, -1.0 / 6, 1.0 / 120, -1.0 / 5040, 1.0 / 362880, -1.0 / 39916800, 1.0 / 6227020800)
MESH = pl.DeviceIdType.MESH
N = 128
X = 32
CHUNKS = 4
CX = X // CHUNKS
ROWS, RING, CORES, SUBS = 4, 8, 2, 4
f32 = jnp.float32
bf16 = jnp.bfloat16


def sinc_series(square):
    series = jnp.full_like(square, sinc_terms[-1])
    for term in sinc_terms[-2::-1]:
        series = series * square + f32(term)
    return series


def cosine(mode, cell, length):
    extent = jnp.full(mode.shape, length, jnp.int32).astype(f32)
    period = 4.0 * extent
    steps = (mode * (2 * cell + 1)).astype(f32)
    steps = steps - period * jnp.floor(steps / period) - 2.0 * extent
    half = steps * (f32(jnp.pi) / period)
    sine = half * sinc_series(half * half)
    scaling = jnp.sqrt(jnp.where(mode == 0, 1.0, 2.0) / extent)
    value = scaling * (2.0 * (sine * sine) - 1.0)
    return jnp.where((mode < length) & (cell < length), value, 0.0)


def parts_of(value):
    high = value.astype(bf16)
    return high, (value - high.astype(f32)).astype(bf16)


def left_stack(table):
    high, low = parts_of(table)
    return jnp.concatenate(
        [jnp.concatenate([high, high], 1), jnp.concatenate([low, jnp.zeros_like(low)], 1)], 0
    )


def right_stack(table):
    high, low = parts_of(table)
    return jnp.concatenate(
        [jnp.concatenate([high, low], 1), jnp.concatenate([high, jnp.zeros_like(low)], 1)], 0
    )


def times_right(value, stack):
    high, low = parts_of(value)
    out = jnp.dot(jnp.concatenate([high, low], 1), stack, preferred_element_type=f32)
    return out[:, :N] + out[:, N:]


def left_times(stack, pair):
    high, low = parts_of(pair)
    out = jnp.dot(stack, jnp.concatenate([high, low], 0), preferred_element_type=f32)
    return out[:N] + out[N:]


def kernel(
    picks, limits, adj_next, adj_later,
    out_now, out_earlier,
    fields, stage, recv, back, land, stacks, base, by_mode, modes, wave, source,
    faces, face_send, face_in, near_first, near_second, wanted, wanted_in, coup, coup_send, coup_all, coup_modes,
    load_sem, store_sem, local_sem, big_send, big_recv,
    face_ssem, face_rsem, ring_ssem, ring_rsem, core_ssem, core_rsem,
    row_ssem, row_rsem, all_ssem, all_rsem,
):
    row, ring = lax.axis_index("row"), lax.axis_index("z")
    core, sub = lax.axis_index("core"), lax.axis_index("sub")
    inputs = (adj_next, adj_later)
    outputs = (out_now, out_earlier)
    recv_flat = [recv.at[i].reshape(N * X, N) for i in range(2)]
    back_flat = [back.at[i].reshape(N * X, N) for i in range(2)]
    near = (near_first, near_second)
    sent = []

    def load(i, c):
        return pltpu.make_async_copy(
            inputs[i].at[0, pl.ds(CX * c, CX)], fields.at[i, pl.ds(CX * c, CX)], load_sem.at[i, c]
        )

    for i in range(2):
        for c in range(CHUNKS):
            load(i, c).start()

    barrier = pltpu.get_barrier_semaphore()
    for j in (1, 2, 3):
        pl.semaphore_signal(barrier, inc=1, device_id={"sub": lax.rem(sub + j, SUBS)}, device_id_type=MESH)
        pl.semaphore_signal(barrier, inc=1, device_id={"row": lax.rem(row + j, ROWS)}, device_id_type=MESH)
    for j in (1, RING - 1):
        pl.semaphore_signal(barrier, inc=1, device_id={"z": lax.rem(ring + j, RING)}, device_id_type=MESH)
    pl.semaphore_signal(barrier, inc=1, device_id={"core": 1 - core}, device_id_type=MESH)

    place = ring * CORES + core
    plane = RING * CORES

    len_x, len_y = picks[96], picks[97]
    down = lax.broadcasted_iota(jnp.int32, (N, N), 0)
    across = lax.broadcasted_iota(jnp.int32, (N, N), 1)
    stacks[2] = left_stack(cosine(down, across, len_y))
    stacks[4] = right_stack(cosine(across, down, N))

    def other_tables():
        stacks[0] = left_stack(cosine(down, across, len_x))
        stacks[1] = left_stack(cosine(across, down, len_x))
        stacks[3] = left_stack(cosine(across, down, len_y))
        stacks[5] = right_stack(cosine(down, across, N))
        quarter = f32((jnp.pi * time_step / 2) ** 2)
        ratio_x = down.astype(f32) / jnp.full((N, N), len_x, jnp.int32).astype(f32)
        ratio_z = across.astype(f32) / f32(N)
        base[...] = quarter * (ratio_x * ratio_x + ratio_z * ratio_z)
        index = lax.broadcasted_iota(jnp.int32, (8 * X, N), 0)
        mode, kind = sub * X + (index >> 3), index & 7
        cell = jnp.where(kind < 3, kind, len_y - 6 + kind)
        ratio_y = mode.astype(f32) / jnp.full((8 * X, N), len_y, jnp.int32).astype(f32)
        by_mode[...] = jnp.where(kind < 6, cosine(mode, cell, len_y), quarter * (ratio_y * ratio_y))

    other_tables()
    def per_mode(l, kind):
        return jnp.broadcast_to(by_mode[pl.ds(8 * l + kind, 1), :], (N, N))

    pl.semaphore_wait(barrier, 9)

    def remote(src, dst, ssem, rsem, where):
        copy = pltpu.make_async_remote_copy(
            src_ref=src, dst_ref=dst, send_sem=ssem, recv_sem=rsem, device_id=where, device_id_type=MESH
        )
        return copy

    def post(copy):
        copy.start()
        sent.append(copy)

    def large(a, c, j):
        d = lax.rem(sub + j, SUBS)
        if a < 2:
            src = stage.at[a, pl.ds(CX * c, CX), pl.ds(X * d, X), :]
            dst = recv.at[a, pl.ds(X * sub + CX * c, CX)]
        else:
            src = back.at[a - 2, pl.ds(X * d + CX * c, CX)]
            dst = land.at[a - 2, pl.ds(CX * c, CX), pl.ds(X * sub, X), :]
        return src, dst, d

    def large_copy(a, c, j):
        src, dst, d = large(a, c, j)
        if j == 0:
            return pltpu.make_async_copy(src, dst, local_sem.at[a, c])
        return remote(src, dst, big_send.at[a, c, j - 1], big_recv.at[a, c, j - 1], {"sub": d})

    def large_start(a, c):
        for j in (2, 1, 3):
            post(large_copy(a, c, j))
        large_copy(a, c, 0).start()

    def large_wait(a, c):
        large_copy(a, c, 0).wait()
        for j in (1, 3, 2):
            large_copy(a, c, j).wait_recv()

    def forward_chunk(i, c):
        def step(p, carry):
            x0 = CX * c + 2 * p
            value = times_right(fields[i, pl.ds(x0, 2)].reshape(2 * N, N), stacks[4])
            value = left_times(stacks[2], jnp.concatenate([value[:N], value[N:]], 1))
            stage[i, x0] = value[:, :N]
            stage[i, x0 + 1] = value[:, N:]
            return carry

        lax.fori_loop(0, CX // 2, step, 0, unroll=2)

    def to_modes(i, l0):
        pair = jnp.concatenate(
            [
                recv_flat[i][pl.ds(l0, N, stride=X), :],
                recv_flat[i][pl.ds(l0 + 1, N, stride=X), :],
            ],
            1,
        )
        return left_times(stacks[0], pair)

    def from_modes(i, l0, pair):
        value = left_times(stacks[1], pair)
        back_flat[i][pl.ds(l0, N, stride=X), :] = value[:, :N]
        back_flat[i][pl.ds(l0 + 1, N, stride=X), :] = value[:, N:]

    def add_faces(l0, first, second):
        for r in range(6):
            faces[r] = faces[r] + (per_mode(l0, r) * first + per_mode(l0 + 1, r) * second)

    def face_copy(e, j):
        d = lax.rem(sub + j, SUBS)
        return remote(
            face_send.at[e, :, pl.ds(X * d, X), :],
            face_in.at[e, j - 1],
            face_ssem.at[e, j - 1],
            face_rsem.at[e, j - 1],
            {"sub": d},
        )

    def faces_start(e):
        for r in (0, 2, 4):
            value = left_times(stacks[1], jnp.concatenate([faces[r], faces[r + 1]], 1))
            face_send[e, r] = value[:, :N]
            face_send[e, r + 1] = value[:, N:]
        for j in (2, 1, 3):
            post(face_copy(e, j))

    def slot(k):
        return lax.rem(ring + k + RING, RING) * CORES + core

    def ring_copy(e, h, side):
        owner = -(h - 1) if side == 0 else h - 1
        k = h - 1 if side == 0 else 3 + h
        block = near[e].at[slot(owner)]
        target = lax.rem(ring + (1 if side == 0 else RING - 1), RING)
        return remote(block, block, ring_ssem.at[e, k], ring_rsem.at[e, k], {"z": target})

    def core_copy(e, k):
        owner = -k if k < 5 else k - 4
        block = near[e].at[slot(owner)]
        return remote(block, block, core_ssem.at[e, k], core_rsem.at[e, k], {"core": 1 - core})

    def row_copy(e, j):
        return remote(
            wanted.at[e, j],
            wanted_in.at[e, j - 1],
            row_ssem.at[e, j - 1],
            row_rsem.at[e, j - 1],
            {"row": lax.rem(row + j, ROWS)},
        )

    def exchange(e, fill):
        fill = list(fill)

        def other_work():
            if fill:
                fill.pop(0)()

        other_work()
        for j in (1, 3, 2):
            face_copy(e, j).wait_recv()
        own = face_send[e, :, pl.ds(X * sub, X), :] + face_in[e, 0] + face_in[e, 1] + face_in[e, 2]
        own = times_right(own.reshape(6 * X, N), stacks[5]).reshape(6, X, N)
        near[e][slot(0)] = own
        post(ring_copy(e, 1, 0))
        post(ring_copy(e, 1, 1))
        post(core_copy(e, 0))
        for h in (1, 2, 3, 4):
            other_work()
            ring_copy(e, h, 0).wait_recv()
            if h < 4:
                post(ring_copy(e, h + 1, 0))
            post(core_copy(e, h))
            if h < 4:
                ring_copy(e, h, 1).wait_recv()
                if h < 3:
                    post(ring_copy(e, h + 1, 1))
                post(core_copy(e, 4 + h))
        other_work()
        for k in range(8):
            core_copy(e, k).wait_recv()

        lane = lax.broadcasted_iota(jnp.int32, (3, X, N), 2) // (N // 4)

        def choose(j, carry):
            for face in range(2):
                total = jnp.zeros((3, X, N), f32)
                for seg in range(4):
                    at = 3 * (8 * j + 4 * face + seg)
                    value = near[e][picks[at], 3 * (1 - face) : 3 * (1 - face) + 3]
                    shift = jnp.full((3, X, N), picks[at + 1], jnp.int32)
                    value = jnp.where((shift & 1) == 1, pltpu.roll(value, N // 4, 2), value)
                    value = jnp.where(shift >= 2, pltpu.roll(value, N // 2, 2), value)
                    taken = (lane == seg) & (jnp.full((3, X, N), picks[at + 2], jnp.int32) == 1)
                    total = jnp.where(taken, value, total)
                wanted[e, j, 3 * face : 3 * face + 3] = total
            return carry

        lax.fori_loop(0, ROWS, choose, 0)
        for j in (2, 1, 3):
            post(row_copy(e, j))
        for work in fill:
            work()
        for j in (1, 3, 2):
            row_copy(e, j).wait_recv()
        other = wanted[e, 0] + wanted_in[e, 0] + wanted_in[e, 1] + wanted_in[e, 2]
        own = near[e][slot(0)]
        x_here = sub * X + lax.broadcasted_iota(jnp.int32, (X, N), 0)
        for face in range(2):
            joined = x_here < jnp.broadcast_to(limits[pl.ds(face, 1), :], (X, N))
            values = [other[0], other[1], other[2], own[0], own[1], own[2]]
            if face == 1:
                values = [own[3], own[4], own[5], other[3], other[4], other[5]]
            for i in range(3):
                line = weights[3 * (1 - face) + i]
                term = sum(line[k] * values[k] for k in range(6) if line[k] != 0.0)
                coup[e, 3 * face + i] = jnp.where(joined, term, 0.0)

    y_index = down
    face_rows = [0, 1, 2, len_y - 3, len_y - 2, len_y - 1]

    def finish_chunk(i, c):
        def step(p, carry):
            x0 = CX * c + 2 * p
            value = left_times(stacks[3], jnp.concatenate([land[i, x0], land[i, x0 + 1]], 1))
            value = times_right(jnp.concatenate([value[:, :N], value[:, N:]], 0), stacks[5])
            for q in range(2):
                x = x0 + q
                result = value[N * q : N * q + N]
                inside = (y_index < len_y) & (jnp.full((N, N), sub * X + x, jnp.int32) < len_x)
                result = result - jnp.where(inside, fields[1 - i, x], 0.0)
                extra = jnp.zeros((N, N), f32)
                for r in range(6):
                    line = jnp.broadcast_to(coup[i, r, pl.ds(x, 1), :], (N, N))
                    extra = jnp.where(y_index == face_rows[r], line, extra)
                land[i, x] = result + extra
            return carry

        lax.fori_loop(0, CX // 2, step, 0, unroll=2)
        store(i, c).start()

    def store(i, c):
        return pltpu.make_async_copy(
            land.at[i, pl.ds(CX * c, CX)], outputs[i].at[0, pl.ds(CX * c, CX)], store_sem.at[i, c]
        )

    for c in range(CHUNKS):
        load(0, c).wait()
        forward_chunk(0, c)
        large_start(0, c)
    for c in range(CHUNKS):
        load(1, c).wait()
        forward_chunk(1, c)
        if c == 0:
            large_start(1, 0)

    def factors(l, carry):
        square = base[...] + per_mode(l, 6)
        unit = sinc_series(square)
        unit = unit * unit
        wave[l] = 2.0 - 4.0 * (square * unit)
        source[l] = time_step**2 * unit
        return carry

    lax.fori_loop(0, X, factors, 0, unroll=2)
    for r in range(6):
        faces[r] = jnp.zeros((N, N), f32)
    for c in range(CHUNKS):
        large_wait(0, c)

    def first_modes(p, carry):
        l0 = 2 * p
        value = to_modes(0, l0)
        modes[0, l0] = value[:, :N]
        modes[0, l0 + 1] = value[:, N:]
        add_faces(l0, source[l0] * value[:, :N], source[l0 + 1] * value[:, N:])
        return carry

    lax.fori_loop(0, X // 2, first_modes, 0, unroll=2)
    faces_start(0)
    large_start(1, 1)

    def first_back(p, carry):
        l0 = 2 * p
        pair = jnp.concatenate([wave[l0] * modes[0, l0], wave[l0 + 1] * modes[0, l0 + 1]], 1)
        from_modes(0, l0, pair)
        return carry

    lax.fori_loop(0, X // 2, first_back, 0, unroll=2)

    def start(a, c):
        return lambda: large_start(a, c)

    def later_modes():
        for c in range(CHUNKS):
            large_wait(1, c)

        def step(p, carry):
            l0 = 2 * p
            value = to_modes(1, l0)
            modes[1, l0] = value[:, :N]
            modes[1, l0 + 1] = value[:, N:]
            return carry

        lax.fori_loop(0, X // 2, step, 0, unroll=2)

    exchange(
        0,
        [start(1, 2), start(1, 3), start(2, 0), start(2, 1), start(2, 2), start(2, 3), later_modes],
    )

    def all_copy(j):
        return remote(
            coup_send,
            coup_all.at[:, pl.ds(X * sub, X), :],
            all_ssem.at[j - 1],
            all_rsem.at[j - 1],
            {"sub": lax.rem(sub + j, SUBS)},
        )

    coup_rows = times_right(coup[0].reshape(6 * X, N), stacks[4]).reshape(6, X, N)
    coup_send[...] = coup_rows
    coup_all[:, pl.ds(X * sub, X), :] = coup_rows
    for j in (2, 1, 3):
        post(all_copy(j))
    for r in range(6):
        faces[r] = jnp.zeros((N, N), f32)
    for j in (1, 3, 2):
        all_copy(j).wait_recv()
    for r in (0, 2, 4):
        value = left_times(stacks[0], jnp.concatenate([coup_all[r], coup_all[r + 1]], 1))
        coup_modes[r] = value[:, :N]
        coup_modes[r + 1] = value[:, N:]

    def second_modes(p, carry):
        l0 = 2 * p
        pair = []
        for q in range(2):
            l = l0 + q
            value = wave[l] * modes[0, l] - modes[1, l]
            for r in range(6):
                value = value + per_mode(l, r) * coup_modes[r]
            modes[1, l] = value
            pair.append(value)
        add_faces(l0, source[l0] * pair[0], source[l0 + 1] * pair[1])
        return carry

    lax.fori_loop(0, X // 2, second_modes, 0)
    faces_start(1)

    def second_back(p, carry):
        l0 = 2 * p
        pair = jnp.concatenate([wave[l0] * modes[1, l0], wave[l0 + 1] * modes[1, l0 + 1]], 1)
        from_modes(1, l0, pair)
        return carry

    lax.fori_loop(0, X // 2, second_back, 0, unroll=2)
    for c in range(CHUNKS):
        large_start(3, c)

    def finish(i, c):
        def work():
            large_wait(2 + i, c)
            finish_chunk(i, c)

        return work

    exchange(1, [finish(0, 0), finish(0, 1), finish(0, 2), finish(0, 3)])
    for c in range(CHUNKS):
        finish(1, c)()
    for copy in sent:
        copy.wait_send()
    for i in range(2):
        for c in range(CHUNKS):
            store(i, c).wait()


def local(adj_next, adj_later, box_sizes, holder, partner):
    part_count = holder.shape[0]
    seg_count = partner.shape[2]
    item_count = 2 * seg_count
    plane = RING * CORES
    my_row = lax.axis_index("row")
    my_place = lax.axis_index("z") * CORES + lax.axis_index("core")
    part_ids = jnp.arange(part_count, dtype=jnp.int32)
    row_ids = (my_row + jnp.arange(ROWS, dtype=jnp.int32)) % ROWS
    groups = row_ids * plane + my_place
    row_parts = jnp.sum(jnp.where(holder[None, :] == groups[:, None], part_ids[None, :], 0), axis=1)
    my_part = row_parts[0]
    len_x = box_sizes[my_part, 0]
    len_y = box_sizes[my_part, 1]
    item_ids = jnp.arange(item_count, dtype=jnp.int32)
    link_ids = partner[row_parts].reshape(ROWS, item_count)
    safe_links = jnp.maximum(link_ids, 0)
    peer_part = safe_links // seg_count
    peer_seg = safe_links % seg_count
    peer_group = holder[peer_part]
    shift = (item_ids[None, :] % seg_count - peer_seg) % seg_count
    here = (peer_group // plane == my_row) & (link_ids >= 0)
    picks = jnp.stack([peer_group % plane, shift, here.astype(jnp.int32)], axis=-1)
    picks = jnp.concatenate([picks.reshape(-1), jnp.stack([len_x, len_y])])
    x_limit = jnp.where(link_ids[0] >= 0, jnp.minimum(len_x, box_sizes[peer_part[0], 0]), 0)
    limits = jnp.repeat(x_limit.reshape(2, seg_count), N // seg_count, axis=1)
    limits = jnp.concatenate([limits, jnp.zeros((6, N), jnp.int32)], axis=0)

    vmem = pl.BlockSpec(memory_space=pltpu.VMEM)
    smem = pl.BlockSpec(memory_space=pltpu.SMEM)
    anywhere = pl.BlockSpec(memory_space=pl.ANY)
    block = jax.ShapeDtypeStruct((1, X, N, N), f32)
    dma = pltpu.SemaphoreType.DMA
    return pl.pallas_call(
        kernel,
        out_shape=(block, block),
        in_specs=[smem, vmem, anywhere, anywhere],
        out_specs=(anywhere, anywhere),
        scratch_shapes=[
            pltpu.VMEM((2, X, N, N), f32),
            pltpu.VMEM((2, X, N, N), f32),
            pltpu.VMEM((2, N, X, N), f32),
            pltpu.VMEM((2, N, X, N), f32),
            pltpu.VMEM((2, X, N, N), f32),
            pltpu.VMEM((6, 2 * N, 2 * N), bf16),
            pltpu.VMEM((N, N), f32),
            pltpu.VMEM((8 * X, N), f32),
            pltpu.VMEM((2, X, N, N), f32),
            pltpu.VMEM((X, N, N), f32),
            pltpu.VMEM((X, N, N), f32),
            pltpu.VMEM((6, N, N), f32),
            pltpu.VMEM((2, 6, N, N), f32),
            pltpu.VMEM((2, 3, 6, X, N), f32),
            pltpu.VMEM((RING * CORES, 6, X, N), f32),
            pltpu.VMEM((RING * CORES, 6, X, N), f32),
            pltpu.VMEM((2, ROWS, 6, X, N), f32),
            pltpu.VMEM((2, 3, 6, X, N), f32),
            pltpu.VMEM((2, 6, X, N), f32),
            pltpu.VMEM((6, X, N), f32),
            pltpu.VMEM((6, N, N), f32),
            pltpu.VMEM((6, N, N), f32),
            dma((2, CHUNKS)),
            dma((2, CHUNKS)),
            dma((4, CHUNKS)),
            dma((4, CHUNKS, 3)),
            dma((4, CHUNKS, 3)),
            dma((2, 3)),
            dma((2, 3)),
            dma((2, 7)),
            dma((2, 7)),
            dma((2, 8)),
            dma((2, 8)),
            dma((2, 3)),
            dma((2, 3)),
            dma((3,)),
            dma((3,)),
        ],
        compiler_params=pltpu.CompilerParams(
            collective_id=0, has_side_effects=True, vmem_limit_bytes=64 * 1000 * 1000
        ),
        name="two_steps",
    )(picks, limits, adj_next, adj_later)


def solution(mesh):
    devices = mesh.devices
    split = Mesh(devices.reshape(ROWS, RING, CORES, SUBS), ("row", "z", "core", "sub"))
    field = P(("row", "z", "core"), "sub", None, None)
    return jax.shard_map(
        local,
        mesh=split,
        in_specs=(field, field, P(), P(), P()),
        out_specs=(field, field),
        check_vma=False,
    )
```

```python
import functools

import jax
import jax.numpy as jnp
from jax import lax
from jax.experimental import pallas as pl
from jax.experimental.pallas import tpu as pltpu
from jax.sharding import Mesh
from jax.sharding import PartitionSpec as P

time_step = 0.5
stencil_rows = (
    (0, 0, -2, 2, 0, 0),
    (0, 2, -27, 27, -2, 0),
    (-2, 27, -270, 270, -27, 2),
    (2, -27, 270, -270, 27, -2),
    (0, -2, 27, -27, 2, 0),
    (0, 0, 2, -2, 0, 0),
)
weights = [[stencil_rows[j][i] / 180.0 for j in range(6)] for i in range(6)]
sinc_terms = (1.0, -1.0 / 6, 1.0 / 120, -1.0 / 5040, 1.0 / 362880, -1.0 / 39916800, 1.0 / 6227020800)
MESH = pl.DeviceIdType.MESH
N = 128
X = 32
CHUNKS = 4
CX = X // CHUNKS
ROWS, RING, CORES, SUBS = 4, 8, 2, 4
f32 = jnp.float32
bf16 = jnp.bfloat16


def sinc_series(square):
    series = jnp.full_like(square, sinc_terms[-1])
    for term in sinc_terms[-2::-1]:
        series = series * square + f32(term)
    return series


def cosine(mode, cell, length):
    extent = jnp.full(mode.shape, length, jnp.int32).astype(f32)
    period = 4.0 * extent
    steps = (mode * (2 * cell + 1)).astype(f32)
    steps = steps - period * jnp.floor(steps / period) - 2.0 * extent
    half = steps * (f32(jnp.pi) / period)
    sine = half * sinc_series(half * half)
    scaling = jnp.sqrt(jnp.where(mode == 0, 1.0, 2.0) / extent)
    value = scaling * (2.0 * (sine * sine) - 1.0)
    return jnp.where((mode < length) & (cell < length), value, 0.0)


def parts_of(value):
    high = value.astype(bf16)
    return high, (value - high.astype(f32)).astype(bf16)


def left_stack(table):
    high, low = parts_of(table)
    return jnp.concatenate(
        [jnp.concatenate([high, high], 1), jnp.concatenate([low, jnp.zeros_like(low)], 1)], 0
    )


def right_stack(table):
    high, low = parts_of(table)
    return jnp.concatenate(
        [jnp.concatenate([high, low], 1), jnp.concatenate([high, jnp.zeros_like(low)], 1)], 0
    )


def times_right(value, stack):
    high, low = parts_of(value)
    out = jnp.dot(jnp.concatenate([high, low], 1), stack, preferred_element_type=f32)
    return out[:, :N] + out[:, N:]


def left_times(stack, pair):
    high, low = parts_of(pair)
    out = jnp.dot(stack, jnp.concatenate([high, low], 0), preferred_element_type=f32)
    return out[:N] + out[N:]


def kernel(
    picks, limits, adj_next, adj_later,
    out_now, out_earlier,
    fields, stage, recv, back, land, stacks, base, by_mode, modes, wave, source,
    faces, face_send, face_in, near_first, near_second, wanted, wanted_in, coup, coup_send, coup_all, coup_modes,
    load_sem, store_sem, local_sem, big_send, big_recv,
    face_ssem, face_rsem, ring_ssem, ring_rsem, core_ssem, core_rsem,
    row_ssem, row_rsem, all_ssem, all_rsem,
):
    row, ring = lax.axis_index("row"), lax.axis_index("z")
    core, sub = lax.axis_index("core"), lax.axis_index("sub")
    inputs = (adj_next, adj_later)
    outputs = (out_now, out_earlier)
    recv_flat = [recv.at[i].reshape(N * X, N) for i in range(2)]
    back_flat = [back.at[i].reshape(N * X, N) for i in range(2)]
    near = (near_first, near_second)
    sent = []

    def load(i, c):
        return pltpu.make_async_copy(
            inputs[i].at[0, pl.ds(CX * c, CX)], fields.at[i, pl.ds(CX * c, CX)], load_sem.at[i, c]
        )

    for i in range(2):
        for c in range(CHUNKS):
            load(i, c).start()

    barrier = pltpu.get_barrier_semaphore()
    for j in (1, 2, 3):
        pl.semaphore_signal(barrier, inc=1, device_id={"sub": lax.rem(sub + j, SUBS)}, device_id_type=MESH)
        pl.semaphore_signal(barrier, inc=1, device_id={"row": lax.rem(row + j, ROWS)}, device_id_type=MESH)
    for j in (1, RING - 1):
        pl.semaphore_signal(barrier, inc=1, device_id={"z": lax.rem(ring + j, RING)}, device_id_type=MESH)
    pl.semaphore_signal(barrier, inc=1, device_id={"core": 1 - core}, device_id_type=MESH)

    place = ring * CORES + core
    plane = RING * CORES

    len_x, len_y = picks[96], picks[97]
    down = lax.broadcasted_iota(jnp.int32, (N, N), 0)
    across = lax.broadcasted_iota(jnp.int32, (N, N), 1)
    stacks[2] = left_stack(cosine(down, across, len_y))
    stacks[4] = right_stack(cosine(across, down, N))

    def other_tables():
        stacks[0] = left_stack(cosine(down, across, len_x))
        stacks[1] = left_stack(cosine(across, down, len_x))
        stacks[3] = left_stack(cosine(across, down, len_y))
        stacks[5] = right_stack(cosine(down, across, N))
        quarter = f32((jnp.pi * time_step / 2) ** 2)
        ratio_x = down.astype(f32) / jnp.full((N, N), len_x, jnp.int32).astype(f32)
        ratio_z = across.astype(f32) / f32(N)
        base[...] = quarter * (ratio_x * ratio_x + ratio_z * ratio_z)
        index = lax.broadcasted_iota(jnp.int32, (8 * X, N), 0)
        mode, kind = sub * X + (index >> 3), index & 7
        cell = jnp.where(kind < 3, kind, len_y - 6 + kind)
        ratio_y = mode.astype(f32) / jnp.full((8 * X, N), len_y, jnp.int32).astype(f32)
        by_mode[...] = jnp.where(kind < 6, cosine(mode, cell, len_y), quarter * (ratio_y * ratio_y))

    other_tables()
    def per_mode(l, kind):
        return jnp.broadcast_to(by_mode[pl.ds(8 * l + kind, 1), :], (N, N))

    pl.semaphore_wait(barrier, 9)

    def remote(src, dst, ssem, rsem, where):
        copy = pltpu.make_async_remote_copy(
            src_ref=src, dst_ref=dst, send_sem=ssem, recv_sem=rsem, device_id=where, device_id_type=MESH
        )
        return copy

    def post(copy):
        copy.start()
        sent.append(copy)

    def large(a, c, j):
        d = lax.rem(sub + j, SUBS)
        if a < 2:
            src = stage.at[a, pl.ds(CX * c, CX), pl.ds(X * d, X), :]
            dst = recv.at[a, pl.ds(X * sub + CX * c, CX)]
        else:
            src = back.at[a - 2, pl.ds(X * d + CX * c, CX)]
            dst = land.at[a - 2, pl.ds(CX * c, CX), pl.ds(X * sub, X), :]
        return src, dst, d

    def large_copy(a, c, j):
        src, dst, d = large(a, c, j)
        if j == 0:
            return pltpu.make_async_copy(src, dst, local_sem.at[a, c])
        return remote(src, dst, big_send.at[a, c, j - 1], big_recv.at[a, c, j - 1], {"sub": d})

    def large_start(a, c):
        for j in (2, 1, 3):
            post(large_copy(a, c, j))
        large_copy(a, c, 0).start()

    def large_wait(a, c):
        large_copy(a, c, 0).wait()
        for j in (1, 3, 2):
            large_copy(a, c, j).wait_recv()

    def forward_chunk(i, c):
        def step(p, carry):
            x0 = CX * c + 2 * p
            value = times_right(fields[i, pl.ds(x0, 2)].reshape(2 * N, N), stacks[4])
            value = left_times(stacks[2], jnp.concatenate([value[:N], value[N:]], 1))
            stage[i, x0] = value[:, :N]
            stage[i, x0 + 1] = value[:, N:]
            return carry

        lax.fori_loop(0, CX // 2, step, 0, unroll=2)

    def to_modes(i, l0):
        pair = jnp.concatenate(
            [
                recv_flat[i][pl.ds(l0, N, stride=X), :],
                recv_flat[i][pl.ds(l0 + 1, N, stride=X), :],
            ],
            1,
        )
        return left_times(stacks[0], pair)

    def from_modes(i, l0, pair):
        value = left_times(stacks[1], pair)
        back_flat[i][pl.ds(l0, N, stride=X), :] = value[:, :N]
        back_flat[i][pl.ds(l0 + 1, N, stride=X), :] = value[:, N:]

    def add_faces(l0, first, second):
        for r in range(6):
            faces[r] = faces[r] + (per_mode(l0, r) * first + per_mode(l0 + 1, r) * second)

    def face_copy(e, j):
        d = lax.rem(sub + j, SUBS)
        return remote(
            face_send.at[e, :, pl.ds(X * d, X), :],
            face_in.at[e, j - 1],
            face_ssem.at[e, j - 1],
            face_rsem.at[e, j - 1],
            {"sub": d},
        )

    def faces_start(e):
        for r in (0, 2, 4):
            value = left_times(stacks[1], jnp.concatenate([faces[r], faces[r + 1]], 1))
            face_send[e, r] = value[:, :N]
            face_send[e, r + 1] = value[:, N:]
        for j in (2, 1, 3):
            post(face_copy(e, j))

    def slot(k):
        return lax.rem(ring + k + RING, RING) * CORES + core

    def ring_copy(e, h, side):
        owner = -(h - 1) if side == 0 else h - 1
        k = h - 1 if side == 0 else 3 + h
        block = near[e].at[slot(owner)]
        target = lax.rem(ring + (1 if side == 0 else RING - 1), RING)
        return remote(block, block, ring_ssem.at[e, k], ring_rsem.at[e, k], {"z": target})

    def core_copy(e, k):
        owner = -k if k < 5 else k - 4
        block = near[e].at[slot(owner)]
        return remote(block, block, core_ssem.at[e, k], core_rsem.at[e, k], {"core": 1 - core})

    def row_copy(e, j):
        return remote(
            wanted.at[e, j],
            wanted_in.at[e, j - 1],
            row_ssem.at[e, j - 1],
            row_rsem.at[e, j - 1],
            {"row": lax.rem(row + j, ROWS)},
        )

    def exchange(e, fill):
        fill = list(fill)

        def other_work():
            work = fill.pop(0) if fill else None
            if work:
                work()

        other_work()
        for j in (1, 3, 2):
            face_copy(e, j).wait_recv()
        own = face_send[e, :, pl.ds(X * sub, X), :] + face_in[e, 0] + face_in[e, 1] + face_in[e, 2]
        own = times_right(own.reshape(6 * X, N), stacks[5]).reshape(6, X, N)
        near[e][slot(0)] = own
        post(ring_copy(e, 1, 0))
        post(ring_copy(e, 1, 1))
        post(core_copy(e, 0))
        for h in (1, 2, 3, 4):
            other_work()
            ring_copy(e, h, 0).wait_recv()
            if h < 4:
                post(ring_copy(e, h + 1, 0))
            post(core_copy(e, h))
            if h < 4:
                ring_copy(e, h, 1).wait_recv()
                if h < 3:
                    post(ring_copy(e, h + 1, 1))
                post(core_copy(e, 4 + h))
        other_work()
        for k in range(8):
            core_copy(e, k).wait_recv()

        lane = lax.broadcasted_iota(jnp.int32, (3, X, N), 2) // (N // 4)

        def choose(j, carry):
            for face in range(2):
                total = jnp.zeros((3, X, N), f32)
                for seg in range(4):
                    at = 3 * (8 * j + 4 * face + seg)
                    value = near[e][picks[at], 3 * (1 - face) : 3 * (1 - face) + 3]
                    shift = jnp.full((3, X, N), picks[at + 1], jnp.int32)
                    value = jnp.where((shift & 1) == 1, pltpu.roll(value, N // 4, 2), value)
                    value = jnp.where(shift >= 2, pltpu.roll(value, N // 2, 2), value)
                    taken = (lane == seg) & (jnp.full((3, X, N), picks[at + 2], jnp.int32) == 1)
                    total = jnp.where(taken, value, total)
                wanted[e, j, 3 * face : 3 * face + 3] = total
            return carry

        lax.fori_loop(0, ROWS, choose, 0)
        for j in (2, 1, 3):
            post(row_copy(e, j))
        for work in fill:
            if work:
                work()
        for j in (1, 3, 2):
            row_copy(e, j).wait_recv()
        other = wanted[e, 0] + wanted_in[e, 0] + wanted_in[e, 1] + wanted_in[e, 2]
        own = near[e][slot(0)]
        x_here = sub * X + lax.broadcasted_iota(jnp.int32, (X, N), 0)
        for face in range(2):
            joined = x_here < jnp.broadcast_to(limits[pl.ds(face, 1), :], (X, N))
            values = [other[0], other[1], other[2], own[0], own[1], own[2]]
            if face == 1:
                values = [own[3], own[4], own[5], other[3], other[4], other[5]]
            for i in range(3):
                line = weights[3 * (1 - face) + i]
                term = sum(line[k] * values[k] for k in range(6) if line[k] != 0.0)
                coup[e, 3 * face + i] = jnp.where(joined, term, 0.0)

    y_index = down
    face_rows = [0, 1, 2, len_y - 3, len_y - 2, len_y - 1]

    def finish_chunk(i, c):
        def step(p, carry):
            x0 = CX * c + 2 * p
            value = left_times(stacks[3], jnp.concatenate([land[i, x0], land[i, x0 + 1]], 1))
            value = times_right(jnp.concatenate([value[:, :N], value[:, N:]], 0), stacks[5])
            for q in range(2):
                x = x0 + q
                result = value[N * q : N * q + N]
                inside = (y_index < len_y) & (jnp.full((N, N), sub * X + x, jnp.int32) < len_x)
                result = result - jnp.where(inside, fields[1 - i, x], 0.0)
                extra = jnp.zeros((N, N), f32)
                for r in range(6):
                    line = jnp.broadcast_to(coup[i, r, pl.ds(x, 1), :], (N, N))
                    extra = jnp.where(y_index == face_rows[r], line, extra)
                land[i, x] = result + extra
            return carry

        lax.fori_loop(0, CX // 2, step, 0, unroll=2)
        store(i, c).start()

    def store(i, c):
        return pltpu.make_async_copy(
            land.at[i, pl.ds(CX * c, CX)], outputs[i].at[0, pl.ds(CX * c, CX)], store_sem.at[i, c]
        )

    for c in range(CHUNKS):
        load(0, c).wait()
        forward_chunk(0, c)
        large_start(0, c)
    for c in range(CHUNKS):
        load(1, c).wait()
        forward_chunk(1, c)
        if c == 0:
            large_start(1, 0)

    def factors(l, carry):
        square = base[...] + per_mode(l, 6)
        unit = sinc_series(square)
        unit = unit * unit
        wave[l] = 2.0 - 4.0 * (square * unit)
        source[l] = time_step**2 * unit
        return carry

    lax.fori_loop(0, X, factors, 0, unroll=2)
    for r in range(6):
        faces[r] = jnp.zeros((N, N), f32)
    for c in range(CHUNKS):
        large_wait(0, c)

    def first_modes(p, carry):
        l0 = 2 * p
        value = to_modes(0, l0)
        modes[0, l0] = value[:, :N]
        modes[0, l0 + 1] = value[:, N:]
        add_faces(l0, source[l0] * value[:, :N], source[l0 + 1] * value[:, N:])
        return carry

    lax.fori_loop(0, X // 2, first_modes, 0, unroll=2)
    faces_start(0)
    large_start(1, 1)

    def first_back(p, carry):
        l0 = 2 * p
        pair = jnp.concatenate([wave[l0] * modes[0, l0], wave[l0 + 1] * modes[0, l0 + 1]], 1)
        from_modes(0, l0, pair)
        return carry

    lax.fori_loop(0, X // 2, first_back, 0, unroll=2)

    def start(a, c):
        return lambda: large_start(a, c)

    def later_modes():
        for c in range(CHUNKS):
            large_wait(1, c)

        def step(p, carry):
            l0 = 2 * p
            value = to_modes(1, l0)
            modes[1, l0] = value[:, :N]
            modes[1, l0 + 1] = value[:, N:]
            return carry

        lax.fori_loop(0, X // 2, step, 0, unroll=2)

    exchange(
        0,
        [start(1, 2), None, start(1, 3), None, start(2, 0), start(2, 1), later_modes],
    )

    def all_copy(j):
        return remote(
            coup_send,
            coup_all.at[:, pl.ds(X * sub, X), :],
            all_ssem.at[j - 1],
            all_rsem.at[j - 1],
            {"sub": lax.rem(sub + j, SUBS)},
        )

    coup_rows = times_right(coup[0].reshape(6 * X, N), stacks[4]).reshape(6, X, N)
    coup_send[...] = coup_rows
    coup_all[:, pl.ds(X * sub, X), :] = coup_rows
    for j in (2, 1, 3):
        post(all_copy(j))
    large_start(2, 2)
    for r in range(6):
        faces[r] = jnp.zeros((N, N), f32)
    for j in (1, 3, 2):
        all_copy(j).wait_recv()
    for r in (0, 2, 4):
        value = left_times(stacks[0], jnp.concatenate([coup_all[r], coup_all[r + 1]], 1))
        coup_modes[r] = value[:, :N]
        coup_modes[r + 1] = value[:, N:]

    def second_modes(p, carry):
        l0 = 2 * p
        pair = []
        for q in range(2):
            l = l0 + q
            value = wave[l] * modes[0, l] - modes[1, l]
            for r in range(6):
                value = value + per_mode(l, r) * coup_modes[r]
            modes[1, l] = value
            pair.append(value)
        add_faces(l0, source[l0] * pair[0], source[l0 + 1] * pair[1])
        return carry

    lax.fori_loop(0, X // 2, second_modes, 0)
    faces_start(1)

    def second_back(p, carry):
        l0 = 2 * p
        pair = jnp.concatenate([wave[l0] * modes[1, l0], wave[l0 + 1] * modes[1, l0 + 1]], 1)
        from_modes(1, l0, pair)
        return carry

    lax.fori_loop(0, X // 2, second_back, 0, unroll=2)
    large_start(2, 3)
    for c in range(CHUNKS):
        large_start(3, c)

    def finish(i, c):
        def work():
            large_wait(2 + i, c)
            finish_chunk(i, c)

        return work

    exchange(1, [None, finish(0, 0), finish(0, 1), finish(0, 2), finish(0, 3)])
    for c in range(CHUNKS):
        finish(1, c)()
    for copy in sent:
        copy.wait_send()
    for i in range(2):
        for c in range(CHUNKS):
            store(i, c).wait()


def plan_kernel(box_sizes, holder, partner, picks, limits):
    row, core, sub = lax.axis_index("row"), lax.axis_index("core"), lax.axis_index("sub")
    plane = RING * CORES
    place = lax.axis_index("z") * CORES + core

    def find(i, found):
        group = holder[i]
        return tuple(
            jnp.where(group == lax.rem(row + j, ROWS) * plane + place, i, found[j]) for j in range(ROWS)
        )

    row_parts = lax.fori_loop(0, holder.shape[0], find, (jnp.int32(0),) * ROWS, unroll=8)
    len_x, len_y = box_sizes[0, row_parts[0]], box_sizes[1, row_parts[0]]
    picks[96] = len_x
    picks[97] = len_y
    for j in range(ROWS):
        for item in range(8):
            link = partner[item // 4, item % 4, row_parts[j]]
            target = jnp.maximum(link, 0)
            group = holder[target >> 2]
            at = 3 * (8 * j + item)
            picks[at] = group & (plane - 1)
            picks[at + 1] = (item - target) & 3
            picks[at + 2] = jnp.where((link >= 0) & ((group >> 4) == row), 1, 0)
    face = lax.broadcasted_iota(jnp.int32, (8, N), 0)
    seg = lax.broadcasted_iota(jnp.int32, (8, N), 1) >> 5
    values = jnp.zeros((8, N), jnp.int32)
    for item in range(8):
        link = partner[item // 4, item % 4, row_parts[0]]
        limit = jnp.minimum(len_x, box_sizes[0, jnp.maximum(link, 0) >> 2])
        here = (face == item // 4) & (seg == item % 4)
        values = jnp.where(here, jnp.where(link >= 0, limit, 0), values)
    limits[...] = values


def local(adj_next, adj_later, box_sizes, holder, partner):
    vmem = pl.BlockSpec(memory_space=pltpu.VMEM)
    smem = pl.BlockSpec(memory_space=pltpu.SMEM)
    anywhere = pl.BlockSpec(memory_space=pl.ANY)
    picks, limits = pl.pallas_call(
        plan_kernel,
        out_shape=(
            jax.ShapeDtypeStruct((128,), jnp.int32),
            jax.ShapeDtypeStruct((8, N), jnp.int32),
        ),
        in_specs=[smem, smem, smem],
        out_specs=(smem, vmem),
        name="plan",
    )(box_sizes.T, holder, jnp.transpose(partner, (1, 2, 0)))
    block = jax.ShapeDtypeStruct((1, X, N, N), f32)
    dma = pltpu.SemaphoreType.DMA
    return pl.pallas_call(
        kernel,
        out_shape=(block, block),
        in_specs=[smem, vmem, anywhere, anywhere],
        out_specs=(anywhere, anywhere),
        scratch_shapes=[
            pltpu.VMEM((2, X, N, N), f32),
            pltpu.VMEM((2, X, N, N), f32),
            pltpu.VMEM((2, N, X, N), f32),
            pltpu.VMEM((2, N, X, N), f32),
            pltpu.VMEM((2, X, N, N), f32),
            pltpu.VMEM((6, 2 * N, 2 * N), bf16),
            pltpu.VMEM((N, N), f32),
            pltpu.VMEM((8 * X, N), f32),
            pltpu.VMEM((2, X, N, N), f32),
            pltpu.VMEM((X, N, N), f32),
            pltpu.VMEM((X, N, N), f32),
            pltpu.VMEM((6, N, N), f32),
            pltpu.VMEM((2, 6, N, N), f32),
            pltpu.VMEM((2, 3, 6, X, N), f32),
            pltpu.VMEM((RING * CORES, 6, X, N), f32),
            pltpu.VMEM((RING * CORES, 6, X, N), f32),
            pltpu.VMEM((2, ROWS, 6, X, N), f32),
            pltpu.VMEM((2, 3, 6, X, N), f32),
            pltpu.VMEM((2, 6, X, N), f32),
            pltpu.VMEM((6, X, N), f32),
            pltpu.VMEM((6, N, N), f32),
            pltpu.VMEM((6, N, N), f32),
            dma((2, CHUNKS)),
            dma((2, CHUNKS)),
            dma((4, CHUNKS)),
            dma((4, CHUNKS, 3)),
            dma((4, CHUNKS, 3)),
            dma((2, 3)),
            dma((2, 3)),
            dma((2, 7)),
            dma((2, 7)),
            dma((2, 8)),
            dma((2, 8)),
            dma((2, 3)),
            dma((2, 3)),
            dma((3,)),
            dma((3,)),
        ],
        compiler_params=pltpu.CompilerParams(
            collective_id=0, has_side_effects=True, vmem_limit_bytes=64 * 1000 * 1000
        ),
        name="two_steps",
    )(picks, limits, adj_next, adj_later)


def solution(mesh):
    devices = mesh.devices
    split = Mesh(devices.reshape(ROWS, RING, CORES, SUBS), ("row", "z", "core", "sub"))
    field = P(("row", "z", "core"), "sub", None, None)
    return jax.shard_map(
        local,
        mesh=split,
        in_specs=(field, field, P(), P(), P()),
        out_specs=(field, field),
        check_vma=False,
    )
```

```python
import functools

import jax
import jax.numpy as jnp
from jax import lax
from jax.experimental import pallas as pl
from jax.experimental.pallas import tpu as pltpu
from jax.sharding import Mesh
from jax.sharding import PartitionSpec as P

time_step = 0.5
stencil_rows = (
    (0, 0, -2, 2, 0, 0),
    (0, 2, -27, 27, -2, 0),
    (-2, 27, -270, 270, -27, 2),
    (2, -27, 270, -270, 27, -2),
    (0, -2, 27, -27, 2, 0),
    (0, 0, 2, -2, 0, 0),
)
weights = [[stencil_rows[j][i] / 180.0 for j in range(6)] for i in range(6)]
sinc_terms = (1.0, -1.0 / 6, 1.0 / 120, -1.0 / 5040, 1.0 / 362880, -1.0 / 39916800, 1.0 / 6227020800)
MESH = pl.DeviceIdType.MESH
N = 128
X = 32
CHUNKS = 4
CX = X // CHUNKS
ROWS, RING, CORES, SUBS = 4, 8, 2, 4
f32 = jnp.float32
bf16 = jnp.bfloat16


def sinc_series(square):
    series = jnp.full_like(square, sinc_terms[-1])
    for term in sinc_terms[-2::-1]:
        series = series * square + f32(term)
    return series


def cosine(mode, cell, length):
    extent = jnp.full(mode.shape, length, jnp.int32).astype(f32)
    period = 4.0 * extent
    steps = (mode * (2 * cell + 1)).astype(f32)
    steps = steps - period * jnp.floor(steps / period) - 2.0 * extent
    half = steps * (f32(jnp.pi) / period)
    sine = half * sinc_series(half * half)
    scaling = jnp.sqrt(jnp.where(mode == 0, 1.0, 2.0) / extent)
    value = scaling * (2.0 * (sine * sine) - 1.0)
    return jnp.where((mode < length) & (cell < length), value, 0.0)


def parts_of(value):
    high = value.astype(bf16)
    return high, (value - high.astype(f32)).astype(bf16)


def left_stack(table):
    high, low = parts_of(table)
    return jnp.concatenate(
        [jnp.concatenate([high, high], 1), jnp.concatenate([low, jnp.zeros_like(low)], 1)], 0
    )


def right_stack(table):
    high, low = parts_of(table)
    return jnp.concatenate(
        [jnp.concatenate([high, low], 1), jnp.concatenate([high, jnp.zeros_like(low)], 1)], 0
    )


def times_right(value, stack):
    high, low = parts_of(value)
    out = jnp.dot(jnp.concatenate([high, low], 1), stack, preferred_element_type=f32)
    return out[:, :N] + out[:, N:]


def left_times(stack, pair):
    high, low = parts_of(pair)
    out = jnp.dot(stack, jnp.concatenate([high, low], 0), preferred_element_type=f32)
    return out[:N] + out[N:]


def kernel(
    picks, limits, adj_next, adj_later,
    out_now, out_earlier,
    fields, stage, recv, back, land, stacks, base, by_mode, modes, wave, source,
    faces, face_send, face_in, near_first, near_second, wanted, wanted_in, coup, coup_send, coup_all, coup_modes,
    load_sem, store_sem, local_sem, big_send, big_recv,
    face_ssem, face_rsem, ring_ssem, ring_rsem, core_ssem, core_rsem,
    row_ssem, row_rsem, all_ssem, all_rsem,
):
    row, ring = lax.axis_index("row"), lax.axis_index("z")
    core, sub = lax.axis_index("core"), lax.axis_index("sub")
    inputs = (adj_next, adj_later)
    outputs = (out_now, out_earlier)
    recv_flat = [recv.at[i].reshape(N * X, N) for i in range(2)]
    back_flat = [back.at[i].reshape(N * X, N) for i in range(2)]
    near = (near_first, near_second)
    sent = []

    def load(i, c):
        return pltpu.make_async_copy(
            inputs[i].at[0, pl.ds(CX * c, CX)], fields.at[i, pl.ds(CX * c, CX)], load_sem.at[i, c]
        )

    for i in range(2):
        for c in range(CHUNKS):
            load(i, c).start()

    barrier = pltpu.get_barrier_semaphore()
    for j in (1, 2, 3):
        pl.semaphore_signal(barrier, inc=1, device_id={"sub": lax.rem(sub + j, SUBS)}, device_id_type=MESH)
        pl.semaphore_signal(barrier, inc=1, device_id={"row": lax.rem(row + j, ROWS)}, device_id_type=MESH)
    for j in (1, RING - 1):
        pl.semaphore_signal(barrier, inc=1, device_id={"z": lax.rem(ring + j, RING)}, device_id_type=MESH)
    pl.semaphore_signal(barrier, inc=1, device_id={"core": 1 - core}, device_id_type=MESH)

    place = ring * CORES + core
    plane = RING * CORES

    len_x, len_y = picks[96], picks[97]
    down = lax.broadcasted_iota(jnp.int32, (N, N), 0)
    across = lax.broadcasted_iota(jnp.int32, (N, N), 1)
    stacks[2] = left_stack(cosine(down, across, len_y))
    stacks[4] = right_stack(cosine(across, down, N))

    def other_tables():
        stacks[0] = left_stack(cosine(down, across, len_x))
        stacks[1] = left_stack(cosine(across, down, len_x))
        stacks[3] = left_stack(cosine(across, down, len_y))
        stacks[5] = right_stack(cosine(down, across, N))
        quarter = f32((jnp.pi * time_step / 2) ** 2)
        ratio_x = down.astype(f32) / jnp.full((N, N), len_x, jnp.int32).astype(f32)
        ratio_z = across.astype(f32) / f32(N)
        base[...] = quarter * (ratio_x * ratio_x + ratio_z * ratio_z)
        index = lax.broadcasted_iota(jnp.int32, (8 * X, N), 0)
        mode, kind = sub * X + (index >> 3), index & 7
        cell = jnp.where(kind < 3, kind, len_y - 6 + kind)
        ratio_y = mode.astype(f32) / jnp.full((8 * X, N), len_y, jnp.int32).astype(f32)
        by_mode[...] = jnp.where(kind < 6, cosine(mode, cell, len_y), quarter * (ratio_y * ratio_y))

    other_tables()
    def per_mode(l, kind):
        return jnp.broadcast_to(by_mode[pl.ds(8 * l + kind, 1), :], (N, N))

    pl.semaphore_wait(barrier, 9)

    def remote(src, dst, ssem, rsem, where):
        copy = pltpu.make_async_remote_copy(
            src_ref=src, dst_ref=dst, send_sem=ssem, recv_sem=rsem, device_id=where, device_id_type=MESH
        )
        return copy

    def post(copy):
        copy.start()
        sent.append(copy)

    def large(a, c, j):
        d = lax.rem(sub + j, SUBS)
        if a < 2:
            src = stage.at[a, pl.ds(CX * c, CX), pl.ds(X * d, X), :]
            dst = recv.at[a, pl.ds(X * sub + CX * c, CX)]
        else:
            src = back.at[a - 2, pl.ds(X * d + CX * c, CX)]
            dst = land.at[a - 2, pl.ds(CX * c, CX), pl.ds(X * sub, X), :]
        return src, dst, d

    def large_copy(a, c, j):
        src, dst, d = large(a, c, j)
        if j == 0:
            return pltpu.make_async_copy(src, dst, local_sem.at[a, c])
        return remote(src, dst, big_send.at[a, c, j - 1], big_recv.at[a, c, j - 1], {"sub": d})

    def large_start(a, c):
        for j in (2, 1, 3):
            post(large_copy(a, c, j))
        large_copy(a, c, 0).start()

    def large_wait(a, c):
        large_copy(a, c, 0).wait()
        for j in (1, 3, 2):
            large_copy(a, c, j).wait_recv()

    def forward_chunk(i, c):
        def step(p, carry):
            x0 = CX * c + 2 * p
            value = times_right(fields[i, pl.ds(x0, 2)].reshape(2 * N, N), stacks[4])
            value = left_times(stacks[2], jnp.concatenate([value[:N], value[N:]], 1))
            stage[i, x0] = value[:, :N]
            stage[i, x0 + 1] = value[:, N:]
            return carry

        lax.fori_loop(0, CX // 2, step, 0, unroll=2)

    def to_modes(i, l0):
        pair = jnp.concatenate(
            [
                recv_flat[i][pl.ds(l0, N, stride=X), :],
                recv_flat[i][pl.ds(l0 + 1, N, stride=X), :],
            ],
            1,
        )
        return left_times(stacks[0], pair)

    def from_modes(i, l0, pair):
        value = left_times(stacks[1], pair)
        back_flat[i][pl.ds(l0, N, stride=X), :] = value[:, :N]
        back_flat[i][pl.ds(l0 + 1, N, stride=X), :] = value[:, N:]

    def add_faces(l0, first, second):
        for r in range(6):
            faces[r] = faces[r] + (per_mode(l0, r) * first + per_mode(l0 + 1, r) * second)

    def face_copy(e, j):
        d = lax.rem(sub + j, SUBS)
        return remote(
            face_send.at[e, :, pl.ds(X * d, X), :],
            face_in.at[e, j - 1],
            face_ssem.at[e, j - 1],
            face_rsem.at[e, j - 1],
            {"sub": d},
        )

    def faces_start(e):
        for r in (0, 2, 4):
            value = left_times(stacks[1], jnp.concatenate([faces[r], faces[r + 1]], 1))
            face_send[e, r] = value[:, :N]
            face_send[e, r + 1] = value[:, N:]
        for j in (2, 1, 3):
            post(face_copy(e, j))

    def slot(k):
        return lax.rem(ring + k + RING, RING) * CORES + core

    def ring_copy(e, h, side):
        owner = -(h - 1) if side == 0 else h - 1
        k = h - 1 if side == 0 else 3 + h
        block = near[e].at[slot(owner)]
        target = lax.rem(ring + (1 if side == 0 else RING - 1), RING)
        return remote(block, block, ring_ssem.at[e, k], ring_rsem.at[e, k], {"z": target})

    def core_copy(e, k):
        owner = -k if k < 5 else k - 4
        block = near[e].at[slot(owner)]
        return remote(block, block, core_ssem.at[e, k], core_rsem.at[e, k], {"core": 1 - core})

    def row_copy(e, j):
        return remote(
            wanted.at[e, j],
            wanted_in.at[e, j - 1],
            row_ssem.at[e, j - 1],
            row_rsem.at[e, j - 1],
            {"row": lax.rem(row + j, ROWS)},
        )

    def exchange(e, fill):
        fill = list(fill)

        def other_work():
            work = fill.pop(0) if fill else None
            if work:
                work()

        other_work()
        for j in (1, 3, 2):
            face_copy(e, j).wait_recv()
        own = face_send[e, :, pl.ds(X * sub, X), :] + face_in[e, 0] + face_in[e, 1] + face_in[e, 2]
        own = times_right(own.reshape(6 * X, N), stacks[5]).reshape(6, X, N)
        near[e][slot(0)] = own
        post(ring_copy(e, 1, 0))
        post(ring_copy(e, 1, 1))
        post(core_copy(e, 0))
        for h in (1, 2, 3, 4):
            other_work()
            ring_copy(e, h, 0).wait_recv()
            if h < 4:
                post(ring_copy(e, h + 1, 0))
            post(core_copy(e, h))
            if h < 4:
                ring_copy(e, h, 1).wait_recv()
                if h < 3:
                    post(ring_copy(e, h + 1, 1))
                post(core_copy(e, 4 + h))
        other_work()
        for k in range(8):
            core_copy(e, k).wait_recv()

        lane = lax.broadcasted_iota(jnp.int32, (3, X, N), 2) // (N // 4)

        def choose(j, carry):
            for face in range(2):
                total = jnp.zeros((3, X, N), f32)
                for seg in range(4):
                    at = 3 * (8 * j + 4 * face + seg)
                    value = near[e][picks[at], 3 * (1 - face) : 3 * (1 - face) + 3]
                    shift = jnp.full((3, X, N), picks[at + 1], jnp.int32)
                    value = jnp.where((shift & 1) == 1, pltpu.roll(value, N // 4, 2), value)
                    value = jnp.where(shift >= 2, pltpu.roll(value, N // 2, 2), value)
                    taken = (lane == seg) & (jnp.full((3, X, N), picks[at + 2], jnp.int32) == 1)
                    total = jnp.where(taken, value, total)
                wanted[e, j, 3 * face : 3 * face + 3] = total
            return carry

        lax.fori_loop(0, ROWS, choose, 0)
        for j in (2, 1, 3):
            post(row_copy(e, j))
        for work in fill:
            if work:
                work()
        for j in (1, 3, 2):
            row_copy(e, j).wait_recv()
        other = wanted[e, 0] + wanted_in[e, 0] + wanted_in[e, 1] + wanted_in[e, 2]
        own = near[e][slot(0)]
        x_here = sub * X + lax.broadcasted_iota(jnp.int32, (X, N), 0)
        for face in range(2):
            joined = x_here < jnp.broadcast_to(limits[pl.ds(face, 1), :], (X, N))
            values = [other[0], other[1], other[2], own[0], own[1], own[2]]
            if face == 1:
                values = [own[3], own[4], own[5], other[3], other[4], other[5]]
            for i in range(3):
                line = weights[3 * (1 - face) + i]
                term = sum(line[k] * values[k] for k in range(6) if line[k] != 0.0)
                coup[e, 3 * face + i] = jnp.where(joined, term, 0.0)

    y_index = down
    face_rows = [0, 1, 2, len_y - 3, len_y - 2, len_y - 1]

    def coupling_rows(i, x):
        extra = jnp.zeros((N, N), f32)
        for r in range(6):
            line = jnp.broadcast_to(coup[i, r, pl.ds(x, 1), :], (N, N))
            extra = jnp.where(y_index == face_rows[r], line, extra)
        return extra

    def add_coupling(i, c):
        def step(p, carry):
            x = CX * c + p
            land[i, x] = land[i, x] + coupling_rows(i, x)
            return carry

        lax.fori_loop(0, CX, step, 0, unroll=2)
        store(i, c).start()

    def finish_chunk(i, c, coupled):
        def step(p, carry):
            x0 = CX * c + 2 * p
            value = left_times(stacks[3], jnp.concatenate([land[i, x0], land[i, x0 + 1]], 1))
            value = times_right(jnp.concatenate([value[:, :N], value[:, N:]], 0), stacks[5])
            for q in range(2):
                x = x0 + q
                result = value[N * q : N * q + N]
                inside = (y_index < len_y) & (jnp.full((N, N), sub * X + x, jnp.int32) < len_x)
                result = result - jnp.where(inside, fields[1 - i, x], 0.0)
                land[i, x] = result + coupling_rows(i, x) if coupled else result
            return carry

        lax.fori_loop(0, CX // 2, step, 0, unroll=2)
        if coupled:
            store(i, c).start()

    def store(i, c):
        return pltpu.make_async_copy(
            land.at[i, pl.ds(CX * c, CX)], outputs[i].at[0, pl.ds(CX * c, CX)], store_sem.at[i, c]
        )

    for c in range(CHUNKS):
        load(0, c).wait()
        forward_chunk(0, c)
        large_start(0, c)
    for c in range(CHUNKS):
        load(1, c).wait()
        forward_chunk(1, c)
        if c == 0:
            large_start(1, 0)

    def factors(l, carry):
        square = base[...] + per_mode(l, 6)
        unit = sinc_series(square)
        unit = unit * unit
        wave[l] = 2.0 - 4.0 * (square * unit)
        source[l] = time_step**2 * unit
        return carry

    lax.fori_loop(0, X, factors, 0, unroll=2)
    for r in range(6):
        faces[r] = jnp.zeros((N, N), f32)
    for c in range(CHUNKS):
        large_wait(0, c)

    def first_modes(p, carry):
        l0 = 2 * p
        value = to_modes(0, l0)
        modes[0, l0] = value[:, :N]
        modes[0, l0 + 1] = value[:, N:]
        add_faces(l0, source[l0] * value[:, :N], source[l0 + 1] * value[:, N:])
        return carry

    lax.fori_loop(0, X // 2, first_modes, 0, unroll=2)
    faces_start(0)
    large_start(1, 1)

    def first_back(p, carry):
        l0 = 2 * p
        pair = jnp.concatenate([wave[l0] * modes[0, l0], wave[l0 + 1] * modes[0, l0 + 1]], 1)
        from_modes(0, l0, pair)
        return carry

    lax.fori_loop(0, X // 2, first_back, 0, unroll=2)

    def start(a, c):
        return lambda: large_start(a, c)

    def later_modes():
        for c in range(CHUNKS):
            large_wait(1, c)

        def step(p, carry):
            l0 = 2 * p
            value = to_modes(1, l0)
            modes[1, l0] = value[:, :N]
            modes[1, l0 + 1] = value[:, N:]
            return carry

        lax.fori_loop(0, X // 2, step, 0, unroll=2)

    exchange(
        0,
        [start(1, 2), None, start(1, 3), None, start(2, 0), start(2, 1), later_modes],
    )

    def all_copy(j):
        return remote(
            coup_send,
            coup_all.at[:, pl.ds(X * sub, X), :],
            all_ssem.at[j - 1],
            all_rsem.at[j - 1],
            {"sub": lax.rem(sub + j, SUBS)},
        )

    coup_rows = times_right(coup[0].reshape(6 * X, N), stacks[4]).reshape(6, X, N)
    coup_send[...] = coup_rows
    coup_all[:, pl.ds(X * sub, X), :] = coup_rows
    for j in (2, 1, 3):
        post(all_copy(j))
    large_start(2, 2)
    for r in range(6):
        faces[r] = jnp.zeros((N, N), f32)
    for j in (1, 3, 2):
        all_copy(j).wait_recv()
    for r in (0, 2, 4):
        value = left_times(stacks[0], jnp.concatenate([coup_all[r], coup_all[r + 1]], 1))
        coup_modes[r] = value[:, :N]
        coup_modes[r + 1] = value[:, N:]

    def second_modes(p, carry):
        l0 = 2 * p
        pair = []
        for q in range(2):
            l = l0 + q
            value = wave[l] * modes[0, l] - modes[1, l]
            for r in range(6):
                value = value + per_mode(l, r) * coup_modes[r]
            modes[1, l] = value
            pair.append(value)
        add_faces(l0, source[l0] * pair[0], source[l0 + 1] * pair[1])
        return carry

    lax.fori_loop(0, X // 2, second_modes, 0)
    faces_start(1)

    def second_back(p, carry):
        l0 = 2 * p
        pair = jnp.concatenate([wave[l0] * modes[1, l0], wave[l0 + 1] * modes[1, l0 + 1]], 1)
        from_modes(1, l0, pair)
        return carry

    lax.fori_loop(0, X // 2, second_back, 0, unroll=2)
    large_start(2, 3)
    for c in range(CHUNKS):
        large_start(3, c)

    def finish(i, c, coupled=True):
        def work():
            large_wait(2 + i, c)
            finish_chunk(i, c, coupled)

        return work

    exchange(
        1,
        [None, finish(0, 0), finish(0, 1), finish(0, 2), finish(0, 3), None, finish(1, 0, False), finish(1, 1, False)],
    )
    add_coupling(1, 0)
    add_coupling(1, 1)
    finish(1, 2)()
    finish(1, 3)()
    for copy in sent:
        copy.wait_send()
    for i in range(2):
        for c in range(CHUNKS):
            store(i, c).wait()


def plan_kernel(box_sizes, holder, partner, picks, limits):
    row, core, sub = lax.axis_index("row"), lax.axis_index("core"), lax.axis_index("sub")
    plane = RING * CORES
    place = lax.axis_index("z") * CORES + core

    def find(i, found):
        group = holder[i]
        return tuple(
            jnp.where(group == lax.rem(row + j, ROWS) * plane + place, i, found[j]) for j in range(ROWS)
        )

    row_parts = lax.fori_loop(0, holder.shape[0], find, (jnp.int32(0),) * ROWS, unroll=8)
    len_x, len_y = box_sizes[0, row_parts[0]], box_sizes[1, row_parts[0]]
    picks[96] = len_x
    picks[97] = len_y
    for j in range(ROWS):
        for item in range(8):
            link = partner[item // 4, item % 4, row_parts[j]]
            target = jnp.maximum(link, 0)
            group = holder[target >> 2]
            at = 3 * (8 * j + item)
            picks[at] = group & (plane - 1)
            picks[at + 1] = (item - target) & 3
            picks[at + 2] = jnp.where((link >= 0) & ((group >> 4) == row), 1, 0)
    face = lax.broadcasted_iota(jnp.int32, (8, N), 0)
    seg = lax.broadcasted_iota(jnp.int32, (8, N), 1) >> 5
    values = jnp.zeros((8, N), jnp.int32)
    for item in range(8):
        link = partner[item // 4, item % 4, row_parts[0]]
        limit = jnp.minimum(len_x, box_sizes[0, jnp.maximum(link, 0) >> 2])
        here = (face == item // 4) & (seg == item % 4)
        values = jnp.where(here, jnp.where(link >= 0, limit, 0), values)
    limits[...] = values


def local(adj_next, adj_later, box_sizes, holder, partner):
    vmem = pl.BlockSpec(memory_space=pltpu.VMEM)
    smem = pl.BlockSpec(memory_space=pltpu.SMEM)
    anywhere = pl.BlockSpec(memory_space=pl.ANY)
    picks, limits = pl.pallas_call(
        plan_kernel,
        out_shape=(
            jax.ShapeDtypeStruct((128,), jnp.int32),
            jax.ShapeDtypeStruct((8, N), jnp.int32),
        ),
        in_specs=[smem, smem, smem],
        out_specs=(smem, vmem),
        name="plan",
    )(box_sizes.T, holder, jnp.transpose(partner, (1, 2, 0)))
    block = jax.ShapeDtypeStruct((1, X, N, N), f32)
    dma = pltpu.SemaphoreType.DMA
    return pl.pallas_call(
        kernel,
        out_shape=(block, block),
        in_specs=[smem, vmem, anywhere, anywhere],
        out_specs=(anywhere, anywhere),
        scratch_shapes=[
            pltpu.VMEM((2, X, N, N), f32),
            pltpu.VMEM((2, X, N, N), f32),
            pltpu.VMEM((2, N, X, N), f32),
            pltpu.VMEM((2, N, X, N), f32),
            pltpu.VMEM((2, X, N, N), f32),
            pltpu.VMEM((6, 2 * N, 2 * N), bf16),
            pltpu.VMEM((N, N), f32),
            pltpu.VMEM((8 * X, N), f32),
            pltpu.VMEM((2, X, N, N), f32),
            pltpu.VMEM((X, N, N), f32),
            pltpu.VMEM((X, N, N), f32),
            pltpu.VMEM((6, N, N), f32),
            pltpu.VMEM((2, 6, N, N), f32),
            pltpu.VMEM((2, 3, 6, X, N), f32),
            pltpu.VMEM((RING * CORES, 6, X, N), f32),
            pltpu.VMEM((RING * CORES, 6, X, N), f32),
            pltpu.VMEM((2, ROWS, 6, X, N), f32),
            pltpu.VMEM((2, 3, 6, X, N), f32),
            pltpu.VMEM((2, 6, X, N), f32),
            pltpu.VMEM((6, X, N), f32),
            pltpu.VMEM((6, N, N), f32),
            pltpu.VMEM((6, N, N), f32),
            dma((2, CHUNKS)),
            dma((2, CHUNKS)),
            dma((4, CHUNKS)),
            dma((4, CHUNKS, 3)),
            dma((4, CHUNKS, 3)),
            dma((2, 3)),
            dma((2, 3)),
            dma((2, 7)),
            dma((2, 7)),
            dma((2, 8)),
            dma((2, 8)),
            dma((2, 3)),
            dma((2, 3)),
            dma((3,)),
            dma((3,)),
        ],
        compiler_params=pltpu.CompilerParams(
            collective_id=0, has_side_effects=True, vmem_limit_bytes=64 * 1000 * 1000
        ),
        name="two_steps",
    )(picks, limits, adj_next, adj_later)


def solution(mesh):
    devices = mesh.devices
    split = Mesh(devices.reshape(ROWS, RING, CORES, SUBS), ("row", "z", "core", "sub"))
    field = P(("row", "z", "core"), "sub", None, None)
    return jax.shard_map(
        local,
        mesh=split,
        in_specs=(field, field, P(), P(), P()),
        out_specs=(field, field),
        check_vma=False,
    )
```

```python
import functools

import jax
import jax.numpy as jnp
from jax import lax
from jax.experimental import pallas as pl
from jax.experimental.pallas import tpu as pltpu
from jax.sharding import Mesh
from jax.sharding import PartitionSpec as P

time_step = 0.5
stencil_rows = (
    (0, 0, -2, 2, 0, 0),
    (0, 2, -27, 27, -2, 0),
    (-2, 27, -270, 270, -27, 2),
    (2, -27, 270, -270, 27, -2),
    (0, -2, 27, -27, 2, 0),
    (0, 0, 2, -2, 0, 0),
)
weights = [[stencil_rows[j][i] / 180.0 for j in range(6)] for i in range(6)]
sinc_terms = (1.0, -1.0 / 6, 1.0 / 120, -1.0 / 5040, 1.0 / 362880, -1.0 / 39916800, 1.0 / 6227020800)
MESH = pl.DeviceIdType.MESH
N = 128
X = 32
CHUNKS = 4
CX = X // CHUNKS
ROWS, RING, CORES, SUBS = 4, 8, 2, 4
f32 = jnp.float32
bf16 = jnp.bfloat16


def sinc_series(square):
    series = jnp.full_like(square, sinc_terms[-1])
    for term in sinc_terms[-2::-1]:
        series = series * square + f32(term)
    return series


def cosine(mode, cell, length):
    extent = jnp.full(mode.shape, length, jnp.int32).astype(f32)
    period = 4.0 * extent
    steps = (mode * (2 * cell + 1)).astype(f32)
    steps = steps - period * jnp.floor(steps / period) - 2.0 * extent
    half = steps * (f32(jnp.pi) / period)
    sine = half * sinc_series(half * half)
    scaling = jnp.sqrt(jnp.where(mode == 0, 1.0, 2.0) / extent)
    value = scaling * (2.0 * (sine * sine) - 1.0)
    return jnp.where((mode < length) & (cell < length), value, 0.0)


def parts_of(value):
    high = value.astype(bf16)
    return high, (value - high.astype(f32)).astype(bf16)


def left_stack(table):
    high, low = parts_of(table)
    return jnp.concatenate(
        [jnp.concatenate([high, high], 1), jnp.concatenate([low, jnp.zeros_like(low)], 1)], 0
    )


def right_stack(table):
    high, low = parts_of(table)
    return jnp.concatenate(
        [jnp.concatenate([high, low], 1), jnp.concatenate([high, jnp.zeros_like(low)], 1)], 0
    )


def times_right(value, stack):
    high, low = parts_of(value)
    out = jnp.dot(jnp.concatenate([high, low], 1), stack, preferred_element_type=f32)
    return out[:, :N] + out[:, N:]


def left_times(stack, pair):
    high, low = parts_of(pair)
    out = jnp.dot(stack, jnp.concatenate([high, low], 0), preferred_element_type=f32)
    return out[:N] + out[N:]


def kernel(
    picks, limits, adj_next, adj_later,
    out_now, out_earlier,
    fields, stage, recv, back, land, stacks, base, by_mode, modes, wave, source,
    faces, face_send, face_in, near_first, near_second, wanted, wanted_in, coup, coup_send, coup_all, coup_modes,
    load_sem, store_sem, local_sem, big_send, big_recv,
    face_ssem, face_rsem, ring_ssem, ring_rsem, core_ssem, core_rsem,
    row_ssem, row_rsem, all_ssem, all_rsem,
):
    row, ring = lax.axis_index("row"), lax.axis_index("z")
    core, sub = lax.axis_index("core"), lax.axis_index("sub")
    inputs = (adj_next, adj_later)
    outputs = (out_now, out_earlier)
    recv_flat = [recv.at[i].reshape(N * X, N) for i in range(2)]
    back_flat = [back.at[i].reshape(N * X, N) for i in range(2)]
    near = (near_first, near_second)
    sent = []

    def load(i, c):
        return pltpu.make_async_copy(
            inputs[i].at[0, pl.ds(CX * c, CX)], fields.at[i, pl.ds(CX * c, CX)], load_sem.at[i, c]
        )

    for i in range(2):
        for c in range(CHUNKS):
            load(i, c).start()

    barrier = pltpu.get_barrier_semaphore()
    for j in (1, 2, 3):
        pl.semaphore_signal(barrier, inc=1, device_id={"sub": lax.rem(sub + j, SUBS)}, device_id_type=MESH)
        pl.semaphore_signal(barrier, inc=1, device_id={"row": lax.rem(row + j, ROWS)}, device_id_type=MESH)
    for j in (1, RING - 1):
        pl.semaphore_signal(barrier, inc=1, device_id={"z": lax.rem(ring + j, RING)}, device_id_type=MESH)
    pl.semaphore_signal(barrier, inc=1, device_id={"core": 1 - core}, device_id_type=MESH)

    place = ring * CORES + core
    plane = RING * CORES

    len_x, len_y = picks[96], picks[97]
    down = lax.broadcasted_iota(jnp.int32, (N, N), 0)
    across = lax.broadcasted_iota(jnp.int32, (N, N), 1)
    stacks[2] = left_stack(cosine(down, across, len_y))
    stacks[4] = right_stack(cosine(across, down, N))

    def other_tables():
        stacks[0] = left_stack(cosine(down, across, len_x))
        stacks[1] = left_stack(cosine(across, down, len_x))
        stacks[3] = left_stack(cosine(across, down, len_y))
        stacks[5] = right_stack(cosine(down, across, N))
        quarter = f32((jnp.pi * time_step / 2) ** 2)
        ratio_x = down.astype(f32) / jnp.full((N, N), len_x, jnp.int32).astype(f32)
        ratio_z = across.astype(f32) / f32(N)
        base[...] = quarter * (ratio_x * ratio_x + ratio_z * ratio_z)
        index = lax.broadcasted_iota(jnp.int32, (8 * X, N), 0)
        mode, kind = sub * X + (index >> 3), index & 7
        cell = jnp.where(kind < 3, kind, len_y - 6 + kind)
        ratio_y = mode.astype(f32) / jnp.full((8 * X, N), len_y, jnp.int32).astype(f32)
        by_mode[...] = jnp.where(kind < 6, cosine(mode, cell, len_y), quarter * (ratio_y * ratio_y))

    other_tables()
    def per_mode(l, kind):
        return jnp.broadcast_to(by_mode[pl.ds(8 * l + kind, 1), :], (N, N))

    pl.semaphore_wait(barrier, 9)

    def remote(src, dst, ssem, rsem, where):
        copy = pltpu.make_async_remote_copy(
            src_ref=src, dst_ref=dst, send_sem=ssem, recv_sem=rsem, device_id=where, device_id_type=MESH
        )
        return copy

    def post(copy):
        copy.start()
        sent.append(copy)

    def large(a, c, j):
        d = lax.rem(sub + j, SUBS)
        if a < 2:
            src = stage.at[a, pl.ds(CX * c, CX), pl.ds(X * d, X), :]
            dst = recv.at[a, pl.ds(X * sub + CX * c, CX)]
        else:
            src = back.at[a - 2, pl.ds(X * d + CX * c, CX)]
            dst = land.at[a - 2, pl.ds(CX * c, CX), pl.ds(X * sub, X), :]
        return src, dst, d

    def large_copy(a, c, j):
        src, dst, d = large(a, c, j)
        if j == 0:
            return pltpu.make_async_copy(src, dst, local_sem.at[a, c])
        return remote(src, dst, big_send.at[a, c, j - 1], big_recv.at[a, c, j - 1], {"sub": d})

    def large_start(a, c):
        for j in (2, 1, 3):
            post(large_copy(a, c, j))
        large_copy(a, c, 0).start()

    def large_wait(a, c):
        large_copy(a, c, 0).wait()
        for j in (1, 3, 2):
            large_copy(a, c, j).wait_recv()

    def forward_chunk(i, c):
        def step(p, carry):
            x0 = CX * c + 2 * p
            value = times_right(fields[i, pl.ds(x0, 2)].reshape(2 * N, N), stacks[4])
            value = left_times(stacks[2], jnp.concatenate([value[:N], value[N:]], 1))
            stage[i, x0] = value[:, :N]
            stage[i, x0 + 1] = value[:, N:]
            return carry

        lax.fori_loop(0, CX // 2, step, 0, unroll=2)

    def to_modes(i, l0):
        pair = jnp.concatenate(
            [
                recv_flat[i][pl.ds(l0, N, stride=X), :],
                recv_flat[i][pl.ds(l0 + 1, N, stride=X), :],
            ],
            1,
        )
        return left_times(stacks[0], pair)

    def from_modes(i, l0, pair):
        value = left_times(stacks[1], pair)
        back_flat[i][pl.ds(l0, N, stride=X), :] = value[:, :N]
        back_flat[i][pl.ds(l0 + 1, N, stride=X), :] = value[:, N:]

    def add_faces(l0, first, second):
        for r in range(6):
            faces[r] = faces[r] + (per_mode(l0, r) * first + per_mode(l0 + 1, r) * second)

    def face_copy(e, j):
        d = lax.rem(sub + j, SUBS)
        return remote(
            face_send.at[e, :, pl.ds(X * d, X), :],
            face_in.at[e, j - 1],
            face_ssem.at[e, j - 1],
            face_rsem.at[e, j - 1],
            {"sub": d},
        )

    def faces_start(e):
        for r in (0, 2, 4):
            value = left_times(stacks[1], jnp.concatenate([faces[r], faces[r + 1]], 1))
            face_send[e, r] = value[:, :N]
            face_send[e, r + 1] = value[:, N:]
        for j in (2, 1, 3):
            post(face_copy(e, j))

    def slot(k):
        return lax.rem(ring + k + RING, RING) * CORES + core

    def ring_copy(e, h, side):
        owner = -(h - 1) if side == 0 else h - 1
        k = h - 1 if side == 0 else 3 + h
        block = near[e].at[slot(owner)]
        target = lax.rem(ring + (1 if side == 0 else RING - 1), RING)
        return remote(block, block, ring_ssem.at[e, k], ring_rsem.at[e, k], {"z": target})

    def core_copy(e, k):
        owner = -k if k < 5 else k - 4
        block = near[e].at[slot(owner)]
        return remote(block, block, core_ssem.at[e, k], core_rsem.at[e, k], {"core": 1 - core})

    def row_copy(e, j):
        return remote(
            wanted.at[e, j],
            wanted_in.at[e, j - 1],
            row_ssem.at[e, j - 1],
            row_rsem.at[e, j - 1],
            {"row": lax.rem(row + j, ROWS)},
        )

    def exchange(e, fill):
        fill = list(fill)

        def other_work():
            work = fill.pop(0) if fill else None
            if work:
                work()

        other_work()
        for j in (1, 3, 2):
            face_copy(e, j).wait_recv()
        own = face_send[e, :, pl.ds(X * sub, X), :] + face_in[e, 0] + face_in[e, 1] + face_in[e, 2]
        own = times_right(own.reshape(6 * X, N), stacks[5]).reshape(6, X, N)
        near[e][slot(0)] = own
        post(ring_copy(e, 1, 0))
        post(ring_copy(e, 1, 1))
        post(core_copy(e, 0))
        for h in (1, 2, 3, 4):
            other_work()
            ring_copy(e, h, 0).wait_recv()
            if h < 4:
                post(ring_copy(e, h + 1, 0))
            post(core_copy(e, h))
            if h < 4:
                ring_copy(e, h, 1).wait_recv()
                if h < 3:
                    post(ring_copy(e, h + 1, 1))
                post(core_copy(e, 4 + h))
        other_work()
        for k in range(8):
            core_copy(e, k).wait_recv()

        lane = lax.broadcasted_iota(jnp.int32, (3, X, N), 2) // (N // 4)

        def choose(j, carry):
            for face in range(2):
                total = jnp.zeros((3, X, N), f32)
                for seg in range(4):
                    at = 3 * (8 * j + 4 * face + seg)
                    value = near[e][picks[at], 3 * (1 - face) : 3 * (1 - face) + 3]
                    shift = jnp.full((3, X, N), picks[at + 1], jnp.int32)
                    value = jnp.where((shift & 1) == 1, pltpu.roll(value, N // 4, 2), value)
                    value = jnp.where(shift >= 2, pltpu.roll(value, N // 2, 2), value)
                    taken = (lane == seg) & (jnp.full((3, X, N), picks[at + 2], jnp.int32) == 1)
                    total = jnp.where(taken, value, total)
                wanted[e, j, 3 * face : 3 * face + 3] = total
            return carry

        for j in (2, 1, 3):
            choose(j, 0)
            post(row_copy(e, j))
        choose(0, 0)
        for work in fill:
            if work:
                work()
        for j in (1, 3, 2):
            row_copy(e, j).wait_recv()
        other = wanted[e, 0] + wanted_in[e, 0] + wanted_in[e, 1] + wanted_in[e, 2]
        own = near[e][slot(0)]
        x_here = sub * X + lax.broadcasted_iota(jnp.int32, (X, N), 0)
        for face in range(2):
            joined = x_here < jnp.broadcast_to(limits[pl.ds(face, 1), :], (X, N))
            values = [other[0], other[1], other[2], own[0], own[1], own[2]]
            if face == 1:
                values = [own[3], own[4], own[5], other[3], other[4], other[5]]
            for i in range(3):
                line = weights[3 * (1 - face) + i]
                term = sum(line[k] * values[k] for k in range(6) if line[k] != 0.0)
                coup[e, 3 * face + i] = jnp.where(joined, term, 0.0)

    y_index = down
    face_rows = [0, 1, 2, len_y - 3, len_y - 2, len_y - 1]

    def coupling_rows(i, x):
        extra = jnp.zeros((N, N), f32)
        for r in range(6):
            line = jnp.broadcast_to(coup[i, r, pl.ds(x, 1), :], (N, N))
            extra = jnp.where(y_index == face_rows[r], line, extra)
        return extra

    def add_coupling(i, c):
        def step(p, carry):
            x = CX * c + p
            land[i, x] = land[i, x] + coupling_rows(i, x)
            return carry

        lax.fori_loop(0, CX, step, 0, unroll=2)
        store(i, c).start()

    def finish_chunk(i, c, coupled):
        def step(p, carry):
            x0 = CX * c + 2 * p
            value = left_times(stacks[3], jnp.concatenate([land[i, x0], land[i, x0 + 1]], 1))
            value = times_right(jnp.concatenate([value[:, :N], value[:, N:]], 0), stacks[5])
            for q in range(2):
                x = x0 + q
                result = value[N * q : N * q + N]
                inside = (y_index < len_y) & (jnp.full((N, N), sub * X + x, jnp.int32) < len_x)
                result = result - jnp.where(inside, fields[1 - i, x], 0.0)
                land[i, x] = result + coupling_rows(i, x) if coupled else result
            return carry

        lax.fori_loop(0, CX // 2, step, 0, unroll=2)
        if coupled:
            store(i, c).start()

    def store(i, c):
        return pltpu.make_async_copy(
            land.at[i, pl.ds(CX * c, CX)], outputs[i].at[0, pl.ds(CX * c, CX)], store_sem.at[i, c]
        )

    for c in range(CHUNKS):
        load(0, c).wait()
        forward_chunk(0, c)
        large_start(0, c)
    for c in range(CHUNKS):
        load(1, c).wait()
        forward_chunk(1, c)
        if c == 0:
            large_start(1, 0)

    def factors(l, carry):
        square = base[...] + per_mode(l, 6)
        unit = sinc_series(square)
        unit = unit * unit
        wave[l] = 2.0 - 4.0 * (square * unit)
        source[l] = time_step**2 * unit
        return carry

    lax.fori_loop(0, X, factors, 0, unroll=2)
    for r in range(6):
        faces[r] = jnp.zeros((N, N), f32)
    for c in range(CHUNKS):
        large_wait(0, c)

    def first_modes(p, carry):
        l0 = 2 * p
        value = to_modes(0, l0)
        modes[0, l0] = value[:, :N]
        modes[0, l0 + 1] = value[:, N:]
        add_faces(l0, source[l0] * value[:, :N], source[l0 + 1] * value[:, N:])
        return carry

    lax.fori_loop(0, X // 2, first_modes, 0, unroll=2)
    faces_start(0)
    large_start(1, 1)

    def first_back(p, carry):
        l0 = 2 * p
        pair = jnp.concatenate([wave[l0] * modes[0, l0], wave[l0 + 1] * modes[0, l0 + 1]], 1)
        from_modes(0, l0, pair)
        return carry

    lax.fori_loop(0, X // 2, first_back, 0, unroll=2)

    def start(a, c):
        return lambda: large_start(a, c)

    def later_modes():
        for c in range(CHUNKS):
            large_wait(1, c)

        def step(p, carry):
            l0 = 2 * p
            value = to_modes(1, l0)
            modes[1, l0] = value[:, :N]
            modes[1, l0 + 1] = value[:, N:]
            return carry

        lax.fori_loop(0, X // 2, step, 0, unroll=2)

    exchange(
        0,
        [start(1, 2), None, start(1, 3), None, start(2, 0), start(2, 1), later_modes],
    )

    def all_copy(j):
        return remote(
            coup_send,
            coup_all.at[:, pl.ds(X * sub, X), :],
            all_ssem.at[j - 1],
            all_rsem.at[j - 1],
            {"sub": lax.rem(sub + j, SUBS)},
        )

    coup_rows = times_right(coup[0].reshape(6 * X, N), stacks[4]).reshape(6, X, N)
    coup_send[...] = coup_rows
    coup_all[:, pl.ds(X * sub, X), :] = coup_rows
    for j in (2, 1, 3):
        post(all_copy(j))
    large_start(2, 2)
    for r in range(6):
        faces[r] = jnp.zeros((N, N), f32)
    for j in (1, 3, 2):
        all_copy(j).wait_recv()
    for r in (0, 2, 4):
        value = left_times(stacks[0], jnp.concatenate([coup_all[r], coup_all[r + 1]], 1))
        coup_modes[r] = value[:, :N]
        coup_modes[r + 1] = value[:, N:]

    def second_modes(p, carry):
        l0 = 2 * p
        pair = []
        for q in range(2):
            l = l0 + q
            value = wave[l] * modes[0, l] - modes[1, l]
            for r in range(6):
                value = value + per_mode(l, r) * coup_modes[r]
            modes[1, l] = value
            pair.append(value)
        add_faces(l0, source[l0] * pair[0], source[l0 + 1] * pair[1])
        return carry

    lax.fori_loop(0, X // 2, second_modes, 0)
    faces_start(1)

    def second_back(p, carry):
        l0 = 2 * p
        pair = jnp.concatenate([wave[l0] * modes[1, l0], wave[l0 + 1] * modes[1, l0 + 1]], 1)
        from_modes(1, l0, pair)
        return carry

    lax.fori_loop(0, X // 2, second_back, 0, unroll=2)
    large_start(2, 3)
    for c in range(CHUNKS):
        large_start(3, c)

    def finish(i, c, coupled=True):
        def work():
            large_wait(2 + i, c)
            finish_chunk(i, c, coupled)

        return work

    exchange(
        1,
        [None, finish(0, 0), finish(0, 1), finish(0, 2), finish(0, 3), None, finish(1, 0, False), finish(1, 1, False)],
    )
    add_coupling(1, 0)
    add_coupling(1, 1)
    finish(1, 2)()
    finish(1, 3)()
    for copy in sent:
        copy.wait_send()
    for i in range(2):
        for c in range(CHUNKS):
            store(i, c).wait()


def plan_kernel(box_sizes, holder, partner, picks, limits):
    row, core, sub = lax.axis_index("row"), lax.axis_index("core"), lax.axis_index("sub")
    plane = RING * CORES
    place = lax.axis_index("z") * CORES + core

    def find(i, found):
        group = holder[i]
        return tuple(
            jnp.where(group == lax.rem(row + j, ROWS) * plane + place, i, found[j]) for j in range(ROWS)
        )

    row_parts = lax.fori_loop(0, holder.shape[0], find, (jnp.int32(0),) * ROWS, unroll=8)
    len_x, len_y = box_sizes[0, row_parts[0]], box_sizes[1, row_parts[0]]
    picks[96] = len_x
    picks[97] = len_y
    for j in range(ROWS):
        for item in range(8):
            link = partner[item // 4, item % 4, row_parts[j]]
            target = jnp.maximum(link, 0)
            group = holder[target >> 2]
            at = 3 * (8 * j + item)
            picks[at] = group & (plane - 1)
            picks[at + 1] = (item - target) & 3
            picks[at + 2] = jnp.where((link >= 0) & ((group >> 4) == row), 1, 0)
    face = lax.broadcasted_iota(jnp.int32, (8, N), 0)
    seg = lax.broadcasted_iota(jnp.int32, (8, N), 1) >> 5
    values = jnp.zeros((8, N), jnp.int32)
    for item in range(8):
        link = partner[item // 4, item % 4, row_parts[0]]
        limit = jnp.minimum(len_x, box_sizes[0, jnp.maximum(link, 0) >> 2])
        here = (face == item // 4) & (seg == item % 4)
        values = jnp.where(here, jnp.where(link >= 0, limit, 0), values)
    limits[...] = values


def local(adj_next, adj_later, box_sizes, holder, partner):
    vmem = pl.BlockSpec(memory_space=pltpu.VMEM)
    smem = pl.BlockSpec(memory_space=pltpu.SMEM)
    anywhere = pl.BlockSpec(memory_space=pl.ANY)
    picks, limits = pl.pallas_call(
        plan_kernel,
        out_shape=(
            jax.ShapeDtypeStruct((128,), jnp.int32),
            jax.ShapeDtypeStruct((8, N), jnp.int32),
        ),
        in_specs=[smem, smem, smem],
        out_specs=(smem, vmem),
        name="plan",
    )(box_sizes.T, holder, jnp.transpose(partner, (1, 2, 0)))
    block = jax.ShapeDtypeStruct((1, X, N, N), f32)
    dma = pltpu.SemaphoreType.DMA
    return pl.pallas_call(
        kernel,
        out_shape=(block, block),
        in_specs=[smem, vmem, anywhere, anywhere],
        out_specs=(anywhere, anywhere),
        scratch_shapes=[
            pltpu.VMEM((2, X, N, N), f32),
            pltpu.VMEM((2, X, N, N), f32),
            pltpu.VMEM((2, N, X, N), f32),
            pltpu.VMEM((2, N, X, N), f32),
            pltpu.VMEM((2, X, N, N), f32),
            pltpu.VMEM((6, 2 * N, 2 * N), bf16),
            pltpu.VMEM((N, N), f32),
            pltpu.VMEM((8 * X, N), f32),
            pltpu.VMEM((2, X, N, N), f32),
            pltpu.VMEM((X, N, N), f32),
            pltpu.VMEM((X, N, N), f32),
            pltpu.VMEM((6, N, N), f32),
            pltpu.VMEM((2, 6, N, N), f32),
            pltpu.VMEM((2, 3, 6, X, N), f32),
            pltpu.VMEM((RING * CORES, 6, X, N), f32),
            pltpu.VMEM((RING * CORES, 6, X, N), f32),
            pltpu.VMEM((2, ROWS, 6, X, N), f32),
            pltpu.VMEM((2, 3, 6, X, N), f32),
            pltpu.VMEM((2, 6, X, N), f32),
            pltpu.VMEM((6, X, N), f32),
            pltpu.VMEM((6, N, N), f32),
            pltpu.VMEM((6, N, N), f32),
            dma((2, CHUNKS)),
            dma((2, CHUNKS)),
            dma((4, CHUNKS)),
            dma((4, CHUNKS, 3)),
            dma((4, CHUNKS, 3)),
            dma((2, 3)),
            dma((2, 3)),
            dma((2, 7)),
            dma((2, 7)),
            dma((2, 8)),
            dma((2, 8)),
            dma((2, 3)),
            dma((2, 3)),
            dma((3,)),
            dma((3,)),
        ],
        compiler_params=pltpu.CompilerParams(
            collective_id=0, has_side_effects=True, vmem_limit_bytes=64 * 1000 * 1000
        ),
        name="two_steps",
    )(picks, limits, adj_next, adj_later)


def solution(mesh):
    devices = mesh.devices
    split = Mesh(devices.reshape(ROWS, RING, CORES, SUBS), ("row", "z", "core", "sub"))
    field = P(("row", "z", "core"), "sub", None, None)
    return jax.shard_map(
        local,
        mesh=split,
        in_specs=(field, field, P(), P(), P()),
        out_specs=(field, field),
        check_vma=False,
    )
```
